512 devices in a mesh: blk: 128 (over y, z, core), grp: 4 (over x).
Axes of the slice: x: 4, y: 4, z: 16, core: 2. Of those that a mesh axis runs over, the one named last changes fastest.
Arguments:
- spectra: bfloat16 [32768, 4, 1002], P(('blk', 'grp')), may hold values from -6 to 6
- mid_bin: int32 [2, 32768, 64], P(None, ('blk', 'grp')), may hold values from 0 to 127, as said below
- off_bin: int32 [2, 32768, 64], P(None, ('blk', 'grp')), may hold values from 0 to 15
- owner_slot: int32 [2048], replicated, may hold values from 0 to 2047, each once
Outputs:
- stack: float32 [101, 2048], P(None, ('blk', 'grp'))
The draws below stay inside these ranges and needn't reach their ends.
Inputs may be any that keep to these rules, and one draw needn't show every extreme that they name: owner_slot is a permutation of the bin numbers. `mid_bin`: some midpoint bins are named by no pair.
All inputs are finite; a program needn't handle non-finite values.
Results may differ from the reference program's by a relative error of at most 0.0041.
Values may be sent and summed in bfloat16 or wider, within the bound.
A program may use at most 64 MiB of HBM per device.

```python
import jax
import jax.numpy as jnp
from jax import lax

CH = 64
W = 4
F = 501
LAG = 50
ROUNDS = 2
NOFF = 16
NS = 1000
NLAG = 101
NCH = 32768
NB = 2048
NMID = 128
N_BLK = 128
N_GRP = 4


def draw_mid_bin(key, part):
    key_cap = jax.random.fold_in(key, 11)
    key_rank = jax.random.fold_in(key, 12)
    key_middle = jax.random.fold_in(key, 13)
    key_shuffle = jax.random.fold_in(key, 14)
    empty_count = max(1, NMID // 16)
    used_count = NMID - empty_count
    middle = (1 + jax.random.permutation(key_middle, NMID - 2)).astype(jnp.int32)
    ends = jnp.array([0, NMID - 1], jnp.int32)
    used_bins = jnp.concatenate([ends, middle[:NMID - 2 - empty_count]])
    used_bins = used_bins[jax.random.permutation(key_shuffle, used_count)]
    shape = (ROUNDS, NCH, CH)
    ceiling = jax.random.randint(key_cap, shape, 1, used_count + 1)
    ranking = jax.random.randint(key_rank, shape, 0, ceiling)
    drawn = used_bins[ranking]
    drawn = drawn.at[0, 0, 0].set(0).at[0, 0, 1].set(NMID - 1)
    return drawn.astype(jnp.int32)


def with_ends(values, own_key, smallest, high):
    index_at = [jax.random.randint(jax.random.fold_in(own_key, axis), (), 0, length) for axis, length in enumerate(values.shape)]
    main_axis = values.shape.index(max(values.shape))
    beside = index_at[:main_axis] + [(index_at[main_axis] + 1) % values.shape[main_axis]] + index_at[main_axis + 1:]
    return values.at[tuple(index_at)].set(smallest).at[tuple(beside)].set(high)


def block_scale(rng, extent, split, low, top_value):
    factor_of, own = 1.0, jax.random.fold_in(rng, 6)
    for axis_at, shards_of in split:
        steps = jnp.exp(jax.random.uniform(jax.random.fold_in(own, axis_at), (shards_of,), jnp.float32, low / len(split), top_value / len(split)))
        factor_of = factor_of * jnp.repeat(steps, extent[axis_at] // shards_of).reshape([-1 if axis == axis_at else 1 for axis in range(len(extent))])
    return factor_of


def normal_values(key, extent, spread, bound, pieces=(), kind=jnp.bfloat16):
    values = jax.random.normal(key, extent, jnp.float32) * spread
    if len(pieces) > 0:
        values = block_scale(key, extent, pieces, -0.22, 0.18) * values
    return jnp.clip(values, min=-bound, max=bound).astype(kind)


def setup_inputs(seed: int = 0) -> dict:
    seeds = jax.random.split(jax.random.key(seed), 5)
    return {
        "spectra": normal_values(seeds[0], (NCH, W, 2 * F), 1.0, 6.0, ((0, 512),)),
        "mid_bin": draw_mid_bin(jax.random.fold_in(seeds[4], 71), 0),
        "off_bin": with_ends(jax.random.randint(seeds[2], (ROUNDS, NCH, CH), 0, NOFF), jax.random.fold_in(seeds[2], 1), 0, NOFF - 1).astype(jnp.int32),
        "owner_slot": jax.random.permutation(seeds[3], NB).astype(jnp.int32),
    }


def make_kernel():
    freq = jnp.arange(F).astype(jnp.float32)
    lags = (jnp.arange(NLAG) - LAG).astype(jnp.float32)
    angle = 2.0 * jnp.pi * freq[:, None] * lags[None, :] / NS
    weight = jnp.where((freq == 0) | (freq == F - 1), 1.0, 2.0) / jnp.sqrt(jnp.float32(W * F))
    cos_rows = (weight[:, None] * jnp.cos(angle)).astype(jnp.bfloat16)
    sin_rows = (-weight[:, None] * jnp.sin(angle)).astype(jnp.bfloat16)
    return jnp.concatenate([cos_rows, sin_rows], 0)

def cross_corr(own, other, kernel):
    first = own.astype(jnp.float32)
    second = other.astype(jnp.float32)
    real_a, imag_a = (first[..., :F], first[..., F:])
    real_b, imag_b = (second[..., :F], second[..., F:])
    cross_re = jnp.einsum('iwf,jwf->ijf', real_a, real_b) + jnp.einsum('iwf,jwf->ijf', imag_a, imag_b)
    cross_im = jnp.einsum('iwf,jwf->ijf', imag_a, real_b) - jnp.einsum('iwf,jwf->ijf', real_a, imag_b)
    joined = jnp.concatenate([cross_re, cross_im], -1).astype(jnp.bfloat16)
    joined = joined.reshape(CH * CH, 2 * F)
    return jnp.dot(joined, kernel, preferred_element_type=jnp.float32)

def reference(spectra, mid_bin, off_bin, owner_slot):
    kernel = make_kernel()
    blocks = spectra.reshape(N_BLK, N_GRP, CH, W, 2 * F)
    mids = mid_bin.reshape(ROUNDS, N_BLK, N_GRP, CH, CH)
    offs = off_bin.reshape(ROUNDS, N_BLK, N_GRP, CH, CH)

    def step(carry, index):
        sums, counts = carry
        for rnd in range(ROUNDS):
            partner = (index - rnd - 1) % N_BLK
            for grp_id in range(N_GRP):
                own = blocks[index, grp_id]
                other = blocks[partner, grp_id]
                corr = cross_corr(own, other, kernel)
                pos = owner_slot[mids[rnd, index, grp_id] * NOFF + offs[rnd, index, grp_id]].reshape(-1)
                sums = sums + jax.ops.segment_sum(corr, pos, NB)
                counts = counts + jax.ops.segment_sum(jnp.ones((CH * CH,), jnp.float32), pos, NB)
        return ((sums, counts), None)
    init = (jnp.zeros((NB, NLAG), jnp.float32), jnp.zeros((NB,), jnp.float32))
    (sums, counts), _ = lax.scan(step, init, jnp.arange(N_BLK).astype(jnp.int32))
    return (sums / jnp.sqrt(jnp.maximum(counts, 1.0))[:, None]).T
```

```python
import jax
import jax.numpy as jnp
import numpy as np
from jax import lax
from jax.experimental import pallas as pl
from jax.experimental.pallas import tpu as pltpu
from jax.sharding import PartitionSpec as P

LAG=50; NOFF=16
F=501; W=4; FP=512; TL=128; NL=101

def lag_matrix():
    freq=np.arange(F,dtype=np.float32); lags=(np.arange(NL)-LAG).astype(np.float32)
    angle=(np.float32(2.0*np.pi)*freq[:,None]*lags[None,:]/np.float32(2*(F-1))).astype(np.float32)
    w=np.where((freq==0)|(freq==F-1),1.0,2.0).astype(np.float32)/np.sqrt(np.float32(W*F))
    k=np.zeros((2*FP,TL),np.float32)
    k[:F,:NL]=w[:,None]*np.cos(angle)
    k[FP:FP+F,:NL]=-w[:,None]*np.sin(angle)
    return jnp.asarray(k,jnp.bfloat16)

def prep(spectra):
    x=spectra.reshape(4,16,W,2,F).transpose(0,3,2,1,4)
    x=jnp.pad(x,((0,0),)*4+((0,FP-F),))
    return x.reshape(4,8,16,FP)

def prep_idx(mid,off):
    b=mid*NOFF+off
    return b.reshape(2,4,16,4,16).transpose(0,3,1,2,4).reshape(32,256)

def cross_tile(a_ref, b_ref, dst, ib, jcx):
    for ft in range(4):
        sl=pl.ds(ft*128,128)
        B=[b_ref[jcx,k,:,sl].astype(jnp.float32) for k in range(8)]
        for ii in range(16):
            A=[jnp.broadcast_to(a_ref[ib,k,pl.ds(ii,1),sl],(16,128)) for k in range(8)]
            re=None; im=None
            for w in range(4):
                r=A[w]*B[w]+A[4+w]*B[4+w]
                m=A[4+w]*B[w]-A[w]*B[4+w]
                re=r if re is None else re+r
                im=m if im is None else im+m
            dst[pl.ds(ii*16,16),pl.ds(ft*128,128)]=re.astype(jnp.bfloat16)
            dst[pl.ds(ii*16,16),pl.ds(512+ft*128,128)]=im.astype(jnp.bfloat16)

def corr_tile(src, kmat_ref, pos_ref, corrx, t):
    c=jnp.dot(src[...],kmat_ref[...],preferred_element_type=jnp.float32)
    lane=lax.broadcasted_iota(jnp.int32,(256,TL),1)
    c=jnp.where((lane==NL)|(lane==NL+1),1.0,c)
    bit=(pos_ref[pl.ds(t,1),:]&1).astype(jnp.float32)
    mask=jnp.transpose(jnp.broadcast_to(bit,(128,256)))
    hi=c*mask
    row=pl.multiple_of(t*256,256)
    corrx[pl.ds(row,256),pl.ds(0,TL)]=(c-hi).astype(jnp.bfloat16)
    corrx[pl.ds(row,256),pl.ds(TL,TL)]=hi.astype(jnp.bfloat16)

def lookup(bin_ref, tab_ref, pos_ref):
    tab=tab_ref[...]
    lo=(tab&255).astype(jnp.float32); hi=(tab>>8).astype(jnp.float32)
    tt=jnp.concatenate([lo,hi],0).astype(jnp.bfloat16)
    def body(t,_):
        b=bin_ref[pl.ds(t,1),:]
        sub=lax.broadcasted_iota(jnp.int32,(128,256),0)
        oh=jnp.where(sub==(b&127),1.0,0.0).astype(jnp.bfloat16)
        v=jnp.dot(tt,oh,preferred_element_type=jnp.float32)
        full=v[:16]+256.0*v[16:]
        s16=lax.broadcasted_iota(jnp.int32,(16,256),0)
        p=jnp.sum(jnp.where(s16==(b>>7),full,0.0),axis=0,keepdims=True)
        pos_ref[pl.ds(t,1),:]=p.astype(jnp.int32)
        return 0
    lax.fori_loop(0,32,body,0)

def make_onehot(pos_ref, oh_ref, base, rows):
    def body(t,_):
        a=(pos_ref[pl.ds(t,1),:]>>1)-base
        sub=lax.broadcasted_iota(jnp.int32,(rows,256),0)
        v=jnp.where(sub==a,1.0,0.0).astype(jnp.bfloat16)
        oh_ref[:,pl.ds(pl.multiple_of(t*256,256),256)]=v
        return 0
    lax.fori_loop(0,32,body,0)

def kernel(own_ref,oth_ref,bin_ref,tab_ref,kmat_ref,out_ref,a32,cA,cB,corrx,pos_ref,oh_ref):
    a32[...]=own_ref[...].astype(jnp.float32)
    lookup(bin_ref,tab_ref,pos_ref)
    def body(s,_):
        t=2*s
        rc=s//2
        ib=lax.rem(t,4)
        cross_tile(a32,oth_ref,cA,ib,rc)
        corr_tile(cB,kmat_ref,pos_ref,corrx,jnp.maximum(t-1,0))
        cross_tile(a32,oth_ref,cB,ib+1,rc)
        corr_tile(cA,kmat_ref,pos_ref,corrx,t)
        return 0
    lax.fori_loop(0,16,body,0)
    corr_tile(cB,kmat_ref,pos_ref,corrx,31)
    for h in range(2):
        make_onehot(pos_ref,oh_ref,h*512,512)
        out_ref[pl.ds(h*512,512),:]=jnp.dot(oh_ref[...],corrx[...],preferred_element_type=jnp.float32)

def run(own,oth,bins,tab,kmat):
    return pl.pallas_call(kernel,out_shape=jax.ShapeDtypeStruct((1024,256),jnp.float32),
        in_specs=[pl.BlockSpec(memory_space=pltpu.VMEM)]*5,out_specs=pl.BlockSpec(memory_space=pltpu.VMEM),
        scratch_shapes=[pltpu.VMEM((4,8,16,FP),jnp.float32),pltpu.VMEM((256,1024),jnp.bfloat16),pltpu.VMEM((256,1024),jnp.bfloat16),
            pltpu.VMEM((8192,256),jnp.bfloat16),pltpu.VMEM((32,256),jnp.int32),pltpu.VMEM((512,8192),jnp.bfloat16)],
        compiler_params=pltpu.CompilerParams(vmem_limit_bytes=60*2**20),
    )(own,oth,bins,tab,kmat)


def passed_along(value, axis, by):
    size = lax.axis_size(axis)
    return lax.ppermute(value, axis, [(i, (i + by) % size) for i in range(size)])


def shards(spectra, mid_bin, off_bin, owner_slot):
    own = prep(spectra)
    other = jnp.concatenate([passed_along(own, "blk", 1), passed_along(own, "blk", 2)], 0)
    table = owner_slot.reshape(16, 128)
    part = run(own, other, prep_idx(mid_bin, off_bin), table, lag_matrix())
    part = part.reshape(2048, TL)
    total = lax.psum_scatter(part, ("blk", "grp"), scatter_dimension=0, tiled=True)
    number = total[:, NL:NL + 1]
    return (total[:, :NL] / jnp.sqrt(jnp.maximum(number, 1.0))).T


def solution(mesh):
    in_specs = (
        P(("blk", "grp"), None, None),
        P(None, ("blk", "grp"), None),
        P(None, ("blk", "grp"), None),
        P(),
    )
    return jax.shard_map(shards, mesh=mesh, in_specs=in_specs, out_specs=P(None, ("blk", "grp")), check_vma=False)
```

```python
import jax
import jax.numpy as jnp
import numpy as np
from jax import lax
from jax.experimental import pallas as pl
from jax.experimental.pallas import tpu as pltpu
from jax.sharding import PartitionSpec as P

LAG=50; NOFF=16
F=501; W=4; FP=512; TL=128; NL=101

def lag_matrix():
    freq=np.arange(F,dtype=np.float32); lags=(np.arange(NL)-LAG).astype(np.float32)
    angle=(np.float32(2.0*np.pi)*freq[:,None]*lags[None,:]/np.float32(2*(F-1))).astype(np.float32)
    w=np.where((freq==0)|(freq==F-1),1.0,2.0).astype(np.float32)/np.sqrt(np.float32(W*F))
    k=np.zeros((2*FP,TL),np.float32)
    k[:F,:NL]=w[:,None]*np.cos(angle)
    k[FP:FP+F,:NL]=-w[:,None]*np.sin(angle)
    return jnp.asarray(k,jnp.bfloat16)

def prep(spectra):
    x=spectra.reshape(4,16,W,2,F).transpose(0,3,2,1,4)
    x=jnp.pad(x,((0,0),)*4+((0,FP-F),))
    return x.reshape(4,8,16,FP)

def prep_idx(mid,off):
    b=mid*NOFF+off
    return b.reshape(2,4,16,4,16).transpose(0,3,1,2,4).reshape(32,256)

def cross_tile(a_ref, b_ref, dst, ib, jcx):
    for ft in range(4):
        sl=pl.ds(ft*128,128)
        B=[b_ref[jcx,k,:,sl].astype(jnp.float32) for k in range(8)]
        for ii in range(16):
            A=[jnp.broadcast_to(a_ref[ib,k,pl.ds(ii,1),sl],(16,128)) for k in range(8)]
            re=None; im=None
            for w in range(4):
                r=A[w]*B[w]+A[4+w]*B[4+w]
                m=A[4+w]*B[w]-A[w]*B[4+w]
                re=r if re is None else re+r
                im=m if im is None else im+m
            dst[pl.ds(ii*16,16),pl.ds(ft*128,128)]=re.astype(jnp.bfloat16)
            dst[pl.ds(ii*16,16),pl.ds(512+ft*128,128)]=im.astype(jnp.bfloat16)

def corr_tile(src, kmat_ref, pos_ref, corrx, t):
    c=jnp.dot(src[...],kmat_ref[...],preferred_element_type=jnp.float32)
    lane=lax.broadcasted_iota(jnp.int32,(256,TL),1)
    c=jnp.where((lane==NL)|(lane==NL+1),1.0,c)
    bit=(pos_ref[pl.ds(t,1),:]&1).astype(jnp.float32)
    mask=jnp.transpose(jnp.broadcast_to(bit,(128,256)))
    hi=c*mask
    row=pl.multiple_of(t*256,256)
    corrx[pl.ds(row,256),pl.ds(0,TL)]=(c-hi).astype(jnp.bfloat16)
    corrx[pl.ds(row,256),pl.ds(TL,TL)]=hi.astype(jnp.bfloat16)

def lookup(bin_ref, tab_ref, pos_ref):
    tab=tab_ref[...]
    lo=(tab&255).astype(jnp.float32); hi=(tab>>8).astype(jnp.float32)
    tt=jnp.concatenate([lo,hi],0).astype(jnp.bfloat16)
    def body(t,_):
        b=bin_ref[pl.ds(t,1),:]
        sub=lax.broadcasted_iota(jnp.int32,(128,256),0)
        oh=jnp.where(sub==(b&127),1.0,0.0).astype(jnp.bfloat16)
        v=jnp.dot(tt,oh,preferred_element_type=jnp.float32)
        full=v[:16]+256.0*v[16:]
        s16=lax.broadcasted_iota(jnp.int32,(16,256),0)
        p=jnp.sum(jnp.where(s16==(b>>7),full,0.0),axis=0,keepdims=True)
        pos_ref[pl.ds(t,1),:]=p.astype(jnp.int32)
        return 0
    lax.fori_loop(0,32,body,0)

def make_onehot(pos_ref, oh_ref, base, rows):
    def body(t,_):
        a=(pos_ref[pl.ds(t,1),:]>>1)-base
        sub=lax.broadcasted_iota(jnp.int32,(rows,256),0)
        v=jnp.where(sub==a,1.0,0.0).astype(jnp.bfloat16)
        oh_ref[:,pl.ds(pl.multiple_of(t*256,256),256)]=v
        return 0
    lax.fori_loop(0,32,body,0)


NX, NY, NZ = 4, 4, 16
MESH = pl.DeviceIdType.MESH


def place():
    blk = lax.axis_index("blk")
    return lax.axis_index("grp"), blk // (2 * NZ), lax.rem(blk // 2, NZ), lax.rem(blk, 2)


def device(x, y, z, core):
    return {"blk": (y * NZ + z) * 2 + core, "grp": x}


def plane_peer(d):
    x, y, z, core = place()
    return lax.rem(x + d // NY, NX), lax.rem(y + lax.rem(d, NY), NY), z, core


def line_peer(d):
    x, y, z, core = place()
    return x, y, lax.rem(z + d, NZ), core


def greet():
    barrier = pltpu.get_barrier_semaphore()
    x, y, z, core = place()
    pl.semaphore_signal(barrier, inc=1, device_id=device(x, y, z, 1 - core), device_id_type=MESH)

    def plane(d, _):
        pl.semaphore_signal(barrier, inc=1, device_id=device(*plane_peer(d)), device_id_type=MESH)
        return 0

    def line(d, _):
        pl.semaphore_signal(barrier, inc=1, device_id=device(*line_peer(d)), device_id_type=MESH)
        return 0

    lax.fori_loop(1, NX * NY, plane, 0)
    lax.fori_loop(1, NZ, line, 0)


def split_counts(v):
    lane = lax.rem(lax.broadcasted_iota(jnp.int32, v.shape, len(v.shape) - 1), TL)
    high = jnp.floor(v * (1.0 / 128.0)) * 128.0
    return jnp.where(lane == NL, high, jnp.where(lane == NL + 1, v - high, v))


def kernel(own_ref, oth_ref, bin_ref, tab_ref, kmat_ref, out_ref, a32, cA, cB, corrx, pos_ref, oh_ref,
           away, came, keep, plane_out, plane_in, line_out, line_in,
           core_sems, plane_send, plane_recv, line_send, line_recv):
    greet()
    a32[...] = own_ref[...].astype(jnp.float32)
    lookup(bin_ref, tab_ref, pos_ref)

    def body(s, _):
        t = 2 * s
        rc = s // 2
        ib = lax.rem(t, 4)
        cross_tile(a32, oth_ref, cA, ib, rc)
        corr_tile(cB, kmat_ref, pos_ref, corrx, jnp.maximum(t - 1, 0))
        cross_tile(a32, oth_ref, cB, ib + 1, rc)
        corr_tile(cA, kmat_ref, pos_ref, corrx, t)
        return 0

    lax.fori_loop(0, 16, body, 0)
    corr_tile(cB, kmat_ref, pos_ref, corrx, 31)

    x, y, z, core = place()
    make_onehot(pos_ref, oh_ref, (1 - core) * 512, 512)
    away[...] = jnp.dot(oh_ref[...], corrx[...], preferred_element_type=jnp.float32)
    pl.semaphore_wait(pltpu.get_barrier_semaphore(), NX * NY + NZ - 1)
    swap = pltpu.make_async_remote_copy(
        src_ref=away, dst_ref=came, send_sem=core_sems.at[0], recv_sem=core_sems.at[1],
        device_id=device(x, y, z, 1 - core), device_id_type=MESH)
    swap.start()
    make_onehot(pos_ref, oh_ref, core * 512, 512)
    keep[...] = jnp.dot(oh_ref[...], corrx[...], preferred_element_type=jnp.float32).reshape(NX * NY, 32, 2 * TL)
    swap.wait()

    def merge(d, _):
        v = split_counts(keep[d] + came[pl.ds(pl.multiple_of(d * 32, 32), 32), :])
        keep[d] = v
        plane_out[d] = v.astype(jnp.bfloat16)
        return 0

    lax.fori_loop(0, NX * NY, merge, 0)

    def plane_copy(d):
        px, py, pz, pc = plane_peer(d)
        return pltpu.make_async_remote_copy(
            src_ref=plane_out.at[px * NY + py], dst_ref=plane_in.at[d],
            send_sem=plane_send.at[d], recv_sem=plane_recv.at[d],
            device_id=device(px, py, pz, pc), device_id_type=MESH)

    def start_plane(d, _):
        plane_copy(d).start()
        return 0

    lax.fori_loop(1, NX * NY, start_plane, 0)

    def take_plane(d, acc):
        plane_copy(d).wait()
        return acc + plane_in[d].astype(jnp.float32)

    total = lax.fori_loop(1, NX * NY, take_plane, keep[x * NY + y])
    for i in range(NZ):
        line_out[i] = total[2 * i:2 * i + 2]

    def line_copy(d):
        px, py, pz, pc = line_peer(d)
        return pltpu.make_async_remote_copy(
            src_ref=line_out.at[pz], dst_ref=line_in.at[d],
            send_sem=line_send.at[d], recv_sem=line_recv.at[d],
            device_id=device(px, py, pz, pc), device_id_type=MESH)

    def start_line(d, _):
        line_copy(d).start()
        return 0

    lax.fori_loop(1, NZ, start_line, 0)

    def take_line(d, acc):
        line_copy(d).wait()
        return acc + line_in[d]

    out_ref[...] = lax.fori_loop(1, NZ, take_line, line_out[z])


def run(own, oth, bins, tab, kmat):
    vm = lambda s, d: pltpu.VMEM(s, d)
    dma = pltpu.SemaphoreType.DMA
    return pl.pallas_call(
        kernel, out_shape=jax.ShapeDtypeStruct((2, 2 * TL), jnp.float32),
        in_specs=[pl.BlockSpec(memory_space=pltpu.VMEM)] * 5,
        out_specs=pl.BlockSpec(memory_space=pltpu.VMEM),
        scratch_shapes=[
            vm((4, 8, 16, FP), jnp.float32), vm((256, 1024), jnp.bfloat16), vm((256, 1024), jnp.bfloat16),
            vm((8192, 256), jnp.bfloat16), vm((32, 256), jnp.int32), vm((512, 8192), jnp.bfloat16),
            vm((512, 256), jnp.float32), vm((512, 256), jnp.float32), vm((16, 32, 256), jnp.float32),
            vm((16, 32, 256), jnp.bfloat16), vm((16, 32, 256), jnp.bfloat16),
            vm((16, 2, 256), jnp.float32), vm((16, 2, 256), jnp.float32),
            dma((2,)), dma((16,)), dma((16,)), dma((16,)), dma((16,)),
        ],
        compiler_params=pltpu.CompilerParams(
            vmem_limit_bytes=60 * 2**20, collective_id=0, has_side_effects=True),
    )(own, oth, bins, tab, kmat)


def perm_tab(p):
    core, x, y = (p >> 4) & 1, (p >> 2) & 3, p >> 9
    z, k = (p >> 5) & 15, p & 3
    return core * 1024 + x * 256 + y * 64 + z * 4 + k


def passed_along(value, axis, by):
    size = lax.axis_size(axis)
    return lax.ppermute(value, axis, [(i, (i + by) % size) for i in range(size)])


def shards(spectra, mid_bin, off_bin, owner_slot):
    own = prep(spectra)
    other = jnp.concatenate([passed_along(own, "blk", 1), passed_along(own, "blk", 2)], 0)
    table = perm_tab(owner_slot).reshape(16, 128)
    total = run(own, other, prep_idx(mid_bin, off_bin), table, lag_matrix()).reshape(4, TL)
    number = total[:, NL:NL + 1] + total[:, NL + 1:NL + 2]
    return (total[:, :NL] / jnp.sqrt(jnp.maximum(number, 1.0))).T


def solution(mesh):
    in_specs = (
        P(("blk", "grp"), None, None),
        P(None, ("blk", "grp"), None),
        P(None, ("blk", "grp"), None),
        P(),
    )
    return jax.shard_map(shards, mesh=mesh, in_specs=in_specs, out_specs=P(None, ("blk", "grp")), check_vma=False)
```

```python
import jax
import jax.numpy as jnp
import numpy as np
from jax import lax
from jax.experimental import pallas as pl
from jax.experimental.pallas import tpu as pltpu
from jax.sharding import PartitionSpec as P

LAG = 50
NOFF = 16
F = 501
W = 4
FP = 512
TL = 128
NL = 2 * LAG + 1
bf16, f32 = jnp.bfloat16, jnp.float32


def lag_matrix():
    freq = np.arange(F, dtype=np.float32)
    lags = (np.arange(NL) - LAG).astype(np.float32)
    angle = (np.float32(2.0 * np.pi) * freq[:, None] * lags[None, :] / np.float32(2 * (F - 1))).astype(np.float32)
    w = np.where((freq == 0) | (freq == F - 1), 1.0, 2.0).astype(np.float32) / np.sqrt(np.float32(W * F))
    k = np.zeros((TL, 2 * FP), np.float32)
    k[:NL, :F] = (w[:, None] * np.cos(angle)).T
    k[:NL, FP:FP + F] = (-w[:, None] * np.sin(angle)).T
    return jnp.asarray(k, bf16)


def prep(spectra):
    x = spectra.reshape(64, W, 2, F).transpose(1, 2, 0, 3)
    x = jnp.pad(x, ((0, 0),) * 3 + ((0, FP - F),))
    return x.reshape(8, 64, FP)


def prep_tile(x_ref, bt_ref, ag_ref, q):
    lane = lax.broadcasted_iota(jnp.int32, (64, 128), 1)
    xs = []
    for k in range(8):
        x = x_ref[k, :, pl.ds(q * 128, 128)].astype(f32)
        xs.append(x)
        y = jnp.transpose(jnp.concatenate([x, pltpu.roll(x, 96, 1)], 0)).astype(bf16)
        bt_ref[2 * q, pl.ds(k * 32, 32), :] = y[0:32]
        bt_ref[2 * q + 1, pl.ds(k * 32, 32), :] = y[64:96]
    for s in range(4):
        for h in range(2):
            acc = None
            for m in range(4):
                shift = (32 * (m - s)) % 128
                v = xs[4 * h + m]
                v = pltpu.roll(v, shift, 1) if shift else v
                acc = v if acc is None else jnp.where(lane >= 32 * m, v, acc)
            ag_ref[(4 * q + s) * 2 + h] = acc


def weights(u_ref, v_ref, w_ref, gp, sign):
    lane = lax.broadcasted_iota(jnp.int32, (32, 128), 1)
    left = lane < 64
    sgn = jnp.where(left, 1.0, sign)
    for k in range(8):
        u = u_ref[gp, pl.ds(k * 32, 32), :].astype(f32)
        v = v_ref[gp, pl.ds(k * 32, 32), :].astype(f32)
        ur, vr = pltpu.roll(u, 64, 1), pltpu.roll(v, 64, 1)
        for n, val in ((0, jnp.where(left, u, vr)), (1, jnp.where(left, ur, v))):
            w_ref[n, 0, pl.ds(k * 32, 32), :] = val.astype(bf16)
            other = val * sgn if k % 2 == 0 else -(val * sgn)
            w_ref[n, 1, pl.ds((k ^ 1) * 32, 32), :] = other.astype(bf16)


def stage1(ag_ref, w_ref, ct_ref, gp):
    MI = 8
    row = lax.broadcasted_iota(jnp.int32, (32, 128), 0)
    lane = lax.broadcasted_iota(jnp.int32, (32, 128), 1)
    mask = jnp.where((lane & 31) == row, 1.0, 0.0).astype(bf16)

    def body(ib, _):
        for n in range(2):
            w = jnp.concatenate([w_ref[n, 0], w_ref[n, 1]], 1)
            for h in range(MH):
                parts = []
                for ii in range(MI):
                    halves = []
                    for q in range(2):
                        a = ag_ref[(2 * gp + n) * 2 + q, pl.ds((ib * MH + h) * MI + ii, 1), :]
                        a = jnp.broadcast_to(a, (16, 128)).astype(bf16)
                        halves.append(jnp.concatenate([a, a], 0) * mask)
                    parts.append(jnp.concatenate(halves, 1))
                e = jnp.concatenate(parts, 0)
                o = jnp.dot(e, w, preferred_element_type=f32).astype(bf16)
                r0 = pl.multiple_of((2 * gp + n) * 32, 32)
                for ii in range(MI):
                    p = ((ib * MH + h) * MI + ii) // 2
                    ct_ref[ii % 2, p, pl.ds(r0, 32), :] = o[ii * 32:ii * 32 + 32, 0:128]
                    ct_ref[ii % 2, p, pl.ds(r0 + FP, 32), :] = o[ii * 32:ii * 32 + 32, 128:256]
        return 0

    lax.fori_loop(0, 64 // (MI * MH), body, 0)


MH = 4


def stage2(kt_ref, ct_ref, pos_ref, cx_ref):
    sub = lax.broadcasted_iota(jnp.int32, (TL, 128), 0)
    count = (sub == NL) | (sub == NL + 1)

    def body(s, _):
        for u in range(4):
            ip = 4 * s + u
            w = jnp.concatenate([ct_ref[0, ip], ct_ref[1, ip]], 1)
            c = jnp.dot(kt_ref[...], w, preferred_element_type=f32)
            row = pos_ref[pl.ds(ip, 1), :]
            for h in range(2):
                ch = jnp.where(count, 1.0, c[:, h * 128:h * 128 + 128]).astype(bf16)
                bit = (row[:, h * 128:h * 128 + 128] & 1).astype(f32)
                bit = jnp.broadcast_to(bit, (TL, 128)).astype(bf16)
                hi = ch * bit
                cx_ref[h, ip, pl.ds(0, TL), :] = ch - hi
                cx_ref[h, ip, pl.ds(TL, TL), :] = hi
        return 0

    lax.fori_loop(0, 8, body, 0)


def lookup(bin_ref, tab_ref, pos_ref):
    tab = tab_ref[...]
    tt = jnp.concatenate([(tab & 255).astype(f32), (tab >> 8).astype(f32)], 0).astype(bf16)
    sub = lax.broadcasted_iota(jnp.int32, (128, 256), 0)
    s16 = lax.broadcasted_iota(jnp.int32, (16, 256), 0)

    def body(s, _):
        for u in range(8):
            b = bin_ref[pl.ds(8 * s + u, 1), :]
            oh = jnp.where(sub == (b & 127), 1.0, 0.0).astype(bf16)
            v = jnp.dot(tt, oh, preferred_element_type=f32)
            full = v[:16] + 256.0 * v[16:]
            p = jnp.sum(jnp.where(s16 == (b >> 7), full, 0.0), axis=0, keepdims=True)
            pos_ref[pl.ds(8 * s + u, 1), :] = p.astype(jnp.int32)
        return 0

    lax.fori_loop(0, 4, body, 0)


def binning(pos_ref, cx_ref, acc_ref, base):
    sub = lax.broadcasted_iota(jnp.int32, (256, 128), 0).astype(f32).astype(bf16)
    one, zero = jnp.ones((), bf16), jnp.zeros((), bf16)

    def body(s, _):
        lhs, rhs = [], []
        for u in range(KB):
            t = KB * s + u
            row = pos_ref[pl.ds(t, 1), :]
            for q in range(2):
                a = row[:, q * 128:q * 128 + 128] >> 1
                lo, hi = a & 255, a >> 8
                col = []
                for h in range(2):
                    key = jnp.where(hi == base + h, lo, -1).astype(f32)
                    key = jnp.broadcast_to(key, (256, 128)).astype(bf16)
                    col.append(jnp.where(sub == key, one, zero))
                lhs.append(jnp.concatenate(col, 0))
                rhs.append(cx_ref[q, t])
        o = lax.dot_general(jnp.concatenate(lhs, 1), jnp.concatenate(rhs, 1), (((1,), (1,)), ((), ())), preferred_element_type=f32)
        acc_ref[...] = acc_ref[...] + o
        return 0

    acc_ref[...] = jnp.zeros_like(acc_ref)
    lax.fori_loop(0, 32 // KB, body, 0)


KB = 4


NX, NY, NZ = 4, 4, 16
MESH = pl.DeviceIdType.MESH


def place():
    blk = lax.axis_index("blk")
    return lax.axis_index("grp"), blk // (2 * NZ), lax.rem(blk // 2, NZ), lax.rem(blk, 2)


def device(x, y, z, core):
    return {"blk": (y * NZ + z) * 2 + core, "grp": x}


def plane_peer(d):
    x, y, z, core = place()
    return lax.rem(x + d // NY, NX), lax.rem(y + lax.rem(d, NY), NY), z, core


def line_peer(d):
    x, y, z, core = place()
    return x, y, lax.rem(z + d, NZ), core


def chip_neighbour(by, core):
    n = lax.axis_size("blk")
    chip = lax.axis_index("blk") // 2
    return {"blk": lax.rem(chip + by + n // 2, n // 2) * 2 + core, "grp": lax.axis_index("grp")}


def greet():
    barrier = pltpu.get_barrier_semaphore()
    x, y, z, core = place()

    def tell(device_id):
        pl.semaphore_signal(barrier, inc=1, device_id=device_id, device_id_type=MESH)

    tell(device(x, y, z, 1 - core))
    for by in (1, -1):
        for c in range(2):
            tell(chip_neighbour(by, c))

    def plane(d, _):
        tell(device(*plane_peer(d)))
        return 0

    def line(d, _):
        tell(device(*line_peer(d)))
        return 0

    lax.fori_loop(1, NX * NY, plane, 0)
    lax.fori_loop(1, NZ, line, 0)


def split_counts(v):
    lane = lax.rem(lax.broadcasted_iota(jnp.int32, v.shape, len(v.shape) - 1), TL)
    high = jnp.floor(v * (1.0 / 128.0)) * 128.0
    return jnp.where(lane == NL, high, jnp.where(lane == NL + 1, v - high, v))


def remote(src, dst, send, recv, to):
    return pltpu.make_async_remote_copy(
        src_ref=src, dst_ref=dst, send_sem=send, recv_sem=recv, device_id=to, device_id_type=MESH)


def kernel(x_ref, ubin_ref, vbin_ref, tab_ref, kt_ref, out_ref,
           bt, ag, ub, vb, w, ct, cx, vbin, bins, pos, away, came, keep,
           plane_out, plane_in, line_out, line_in,
           bin_sems, send1, send2, fwd_send, u_recv, v_recv,
           core_sems, plane_send, plane_recv, line_send, line_recv):
    greet()
    x, y, z, core = place()
    sibling = device(x, y, z, 1 - core)
    for q in range(4):
        prep_tile(x_ref, bt, ag, q)
    pl.semaphore_wait(pltpu.get_barrier_semaphore(), NX * NY + NZ + 3)

    def bin_copy():
        return remote(vbin_ref, vbin, bin_sems.at[0], bin_sems.at[1], chip_neighbour(-1, 0))

    def up_copy(g):
        return remote(bt.at[g], ub.at[g], send1.at[g], u_recv.at[g], chip_neighbour(1, lax.rem(g, 2)))

    def side_copy(g):
        return remote(bt.at[g], vb.at[g], send1.at[g], v_recv.at[g], sibling)

    def down_copy(g):
        return remote(bt.at[g], vb.at[g], send2.at[g], v_recv.at[g], chip_neighbour(-1, 0))

    def forward(g):
        return remote(ub.at[g], ub.at[g], fwd_send.at[g], u_recv.at[g], sibling)

    @pl.when(core == 0)
    def _():
        bin_copy().start()

        def start(g, _):
            down_copy(g).start()
            side_copy(g).start()
            return 0

        lax.fori_loop(0, 8, start, 0)
        bin_copy().wait()

    @pl.when(core == 1)
    def _():
        def start(g, _):
            up_copy(g).start()
            return 0

        lax.fori_loop(0, 8, start, 0)
        vbin[...] = vbin_ref[...]

    bins[...] = ubin_ref[...] + vbin[...]
    lookup(bins, tab_ref, pos)
    sign = jnp.where(core == 0, -1.0, 1.0)

    def chunk(s, _):
        first = 2 * (s // 2) + core
        g = jnp.where(lax.rem(s, 2) == 0, first, 4 * (s // 2) + 1 - first)
        forward(g).wait_recv()

        @pl.when(lax.rem(s, 2) == 0)
        def _():
            forward(g).start()

        side_copy(g).wait_recv()
        weights(ub, vb, w, g, sign)
        stage1(ag, w, ct, g)
        return 0

    lax.fori_loop(0, 8, chunk, 0)
    stage2(kt_ref, ct, pos, cx)

    binning(pos, cx, away, 2 * (1 - core))
    swap = remote(away, came, core_sems.at[0], core_sems.at[1], sibling)
    swap.start()
    binning(pos, cx, keep, 2 * core)
    swap.wait()

    def merge(d, _):
        rows = pl.ds(pl.multiple_of(d * 32, 32), 32)
        v = split_counts(keep[rows, :] + came[rows, :])
        keep[rows, :] = v
        plane_out[d] = v.astype(bf16)
        return 0

    lax.fori_loop(0, NX * NY, merge, 0)

    def plane_copy(d):
        px, py, pz, pc = plane_peer(d)
        return remote(plane_out.at[px * NY + py], plane_in.at[d], plane_send.at[d], plane_recv.at[d],
                      device(px, py, pz, pc))

    def start_plane(d, _):
        plane_copy(d).start()
        return 0

    lax.fori_loop(1, NX * NY, start_plane, 0)

    def take_plane(d, acc):
        plane_copy(d).wait()
        return acc + plane_in[d].astype(f32)

    mine = keep[pl.ds(pl.multiple_of((x * NY + y) * 32, 32), 32), :]
    total = lax.fori_loop(1, NX * NY, take_plane, mine)
    for i in range(NZ):
        line_out[i] = total[2 * i:2 * i + 2]

    def line_copy(d):
        px, py, pz, pc = line_peer(d)
        return remote(line_out.at[pz], line_in.at[d], line_send.at[d], line_recv.at[d], device(px, py, pz, pc))

    def start_line(d, _):
        line_copy(d).start()
        return 0

    lax.fori_loop(1, NZ, start_line, 0)

    def take_line(d, acc):
        line_copy(d).wait()
        return acc + line_in[d]

    out_ref[...] = lax.fori_loop(1, NZ, take_line, line_out[z])

    @pl.when(core == 0)
    def _():
        def finish(g, _):
            down_copy(g).wait_send()
            side_copy(g).wait_send()
            return 0

        lax.fori_loop(0, 8, finish, 0)

    @pl.when(core == 1)
    def _():
        def finish(g, _):
            up_copy(g).wait_send()
            return 0

        lax.fori_loop(0, 8, finish, 0)

    def finish(s, _):
        forward(2 * s + core).wait_send()
        return 0

    lax.fori_loop(0, 4, finish, 0)


def run(*args):
    vm = pltpu.VMEM
    dma = pltpu.SemaphoreType.DMA
    i32 = jnp.int32
    return pl.pallas_call(
        kernel, out_shape=jax.ShapeDtypeStruct((2, 2 * TL), f32),
        in_specs=[pl.BlockSpec(memory_space=pltpu.VMEM)] * 5,
        out_specs=pl.BlockSpec(memory_space=pltpu.VMEM),
        scratch_shapes=[
            vm((8, 256, 128), bf16), vm((32, 64, 128), f32), vm((8, 256, 128), bf16), vm((8, 256, 128), bf16),
            vm((2, 2, 256, 128), bf16), vm((2, 32, 1024, 128), bf16), vm((2, 32, 256, 128), bf16),
            vm((32, 256), i32), vm((32, 256), i32), vm((32, 256), i32),
            vm((512, 256), f32), vm((512, 256), f32), vm((512, 256), f32),
            vm((16, 32, 256), bf16), vm((16, 32, 256), bf16), vm((16, 2, 256), f32), vm((16, 2, 256), f32),
            dma((2,)), dma((8,)), dma((8,)), dma((8,)), dma((8,)), dma((8,)),
            dma((2,)), dma((16,)), dma((16,)), dma((16,)), dma((16,)),
        ],
        compiler_params=pltpu.CompilerParams(
            vmem_limit_bytes=60 * 2**20, collective_id=0, has_side_effects=True),
    )(*args)


def perm_tab(p):
    core, x, y = (p >> 4) & 1, (p >> 2) & 3, p >> 9
    z, k = (p >> 5) & 15, p & 3
    return core * 1024 + x * 256 + y * 64 + z * 4 + k


def quarters(b, v):
    b = b.reshape(32, 2, 1, 64)
    pad = jnp.zeros_like(b)
    return jnp.concatenate([pad, b] if v else [b, pad], 2).reshape(32, 256)


def shards(spectra, mid_bin, off_bin, owner_slot):
    b = mid_bin * NOFF + off_bin
    upper = lax.rem(lax.axis_index("blk"), 2) == 1
    ubin = quarters(jnp.where(upper, b[1], b[0]), False)
    vbin = quarters(jnp.where(upper, b[0], b[1].T), True)
    table = perm_tab(owner_slot).reshape(16, 128)
    total = run(prep(spectra), ubin, vbin, table, lag_matrix()).reshape(4, TL)
    number = total[:, NL:NL + 1] + total[:, NL + 1:NL + 2]
    return (total[:, :NL] / jnp.sqrt(jnp.maximum(number, 1.0))).T


def solution(mesh):
    in_specs = (
        P(("blk", "grp"), None, None),
        P(None, ("blk", "grp"), None),
        P(None, ("blk", "grp"), None),
        P(),
    )
    return jax.shard_map(shards, mesh=mesh, in_specs=in_specs, out_specs=P(None, ("blk", "grp")), check_vma=False)
```

```python
import jax
import jax.numpy as jnp
import numpy as np
from jax import lax
from jax.experimental import pallas as pl
from jax.experimental.pallas import tpu as pltpu
from jax.sharding import PartitionSpec as P

LAG = 50
NOFF = 16
F = 501
W = 4
FP = 512
TL = 128
NL = 2 * LAG + 1
bf16, f32 = jnp.bfloat16, jnp.float32


def lag_matrix():
    freq = np.arange(F, dtype=np.float32)
    lags = (np.arange(NL) - LAG).astype(np.float32)
    angle = (np.float32(2.0 * np.pi) * freq[:, None] * lags[None, :] / np.float32(2 * (F - 1))).astype(np.float32)
    w = np.where((freq == 0) | (freq == F - 1), 1.0, 2.0).astype(np.float32) / np.sqrt(np.float32(W * F))
    k = np.zeros((TL, 2 * FP), np.float32)
    k[:NL, :F] = (w[:, None] * np.cos(angle)).T
    k[:NL, FP:FP + F] = (-w[:, None] * np.sin(angle)).T
    return jnp.asarray(k, bf16)


def spread(x_ref, rows_ref):
    for i in range(64):
        x = x_ref[i].astype(f32)
        for t in range(8):
            n = min(128, 2 * F - 128 * t)
            rows_ref[t, pl.ds(8 * i, W), pl.ds(0, n)] = x[:, 128 * t:128 * t + n]


def parts(rows_ref, q):
    lane = lax.broadcasted_iota(jnp.int32, (64, 128), 1)
    cut = F - FP + 128
    gap = FP - F
    out = []
    for w in range(W):
        def tile(t):
            return rows_ref[t, pl.ds(w, 64, stride=8), :]

        re = tile(q)
        im = jnp.where(lane < gap, pltpu.roll(tile(q + 3), gap, 1), pltpu.roll(tile(q + 4), gap, 1))
        if q == 3:
            re, im = jnp.where(lane < cut, re, 0.0), jnp.where(lane < cut, im, 0.0)
        out += [re, im]
    return out


def prep_tile(rows_ref, bt_ref, ag_ref, q):
    lane = lax.broadcasted_iota(jnp.int32, (64, 128), 1)
    xs = parts(rows_ref, q)
    for k in range(8):
        x = xs[k]
        y = jnp.transpose(jnp.concatenate([x, pltpu.roll(x, 96, 1)], 0)).astype(bf16)
        bt_ref[2 * q, pl.ds(k * 32, 32), :] = y[0:32]
        bt_ref[2 * q + 1, pl.ds(k * 32, 32), :] = y[64:96]
    for s in range(4):
        for h in range(2):
            acc = None
            for m in range(4):
                shift = (32 * (m - s)) % 128
                v = xs[4 * h + m]
                v = pltpu.roll(v, shift, 1) if shift else v
                acc = v if acc is None else jnp.where(lane >= 32 * m, v, acc)
            ag_ref[(4 * q + s) * 2 + h] = acc


def weights(u_ref, v_ref, w_ref, gp, sign):
    lane = lax.broadcasted_iota(jnp.int32, (32, 128), 1)
    left = lane < 64
    sgn = jnp.where(left, 1.0, sign)
    for k in range(8):
        u = u_ref[gp, pl.ds(k * 32, 32), :].astype(f32)
        v = v_ref[gp, pl.ds(k * 32, 32), :].astype(f32)
        ur, vr = pltpu.roll(u, 64, 1), pltpu.roll(v, 64, 1)
        for n, val in ((0, jnp.where(left, u, vr)), (1, jnp.where(left, ur, v))):
            w_ref[n, 0, pl.ds(k * 32, 32), :] = val.astype(bf16)
            other = val * sgn if k % 2 == 0 else -(val * sgn)
            w_ref[n, 1, pl.ds((k ^ 1) * 32, 32), :] = other.astype(bf16)


def stage1(ag_ref, w_ref, ct_ref, gp):
    MI = 8
    row = lax.broadcasted_iota(jnp.int32, (32, 128), 0)
    lane = lax.broadcasted_iota(jnp.int32, (32, 128), 1)
    mask = jnp.where((lane & 31) == row, 1.0, 0.0).astype(bf16)

    def body(ib, _):
        for n in range(2):
            w = jnp.concatenate([w_ref[n, 0], w_ref[n, 1]], 1)
            for h in range(MH):
                parts = []
                for ii in range(MI):
                    halves = []
                    for q in range(2):
                        a = ag_ref[(2 * gp + n) * 2 + q, pl.ds((ib * MH + h) * MI + ii, 1), :]
                        a = jnp.broadcast_to(a, (16, 128)).astype(bf16)
                        halves.append(jnp.concatenate([a, a], 0) * mask)
                    parts.append(jnp.concatenate(halves, 1))
                e = jnp.concatenate(parts, 0)
                o = jnp.dot(e, w, preferred_element_type=f32).astype(bf16)
                r0 = pl.multiple_of((2 * gp + n) * 32, 32)
                for ii in range(MI):
                    p = ((ib * MH + h) * MI + ii) // 2
                    ct_ref[ii % 2, p, pl.ds(r0, 32), :] = o[ii * 32:ii * 32 + 32, 0:128]
                    ct_ref[ii % 2, p, pl.ds(r0 + FP, 32), :] = o[ii * 32:ii * 32 + 32, 128:256]
        return 0

    lax.fori_loop(0, 64 // (MI * MH), body, 0)


MH = 4


def stage2(kt_ref, ct_ref, pos_ref, cx_ref):
    sub = lax.broadcasted_iota(jnp.int32, (TL, 128), 0)
    count = (sub == NL) | (sub == NL + 1)

    def body(s, _):
        for u in range(4):
            ip = 4 * s + u
            w = jnp.concatenate([ct_ref[0, ip], ct_ref[1, ip]], 1)
            c = jnp.dot(kt_ref[...], w, preferred_element_type=f32)
            for h in range(2):
                row = pos_ref[pl.ds(2 * ip + h, 1), :]
                ch = jnp.where(count, 1.0, c[:, h * 128:h * 128 + 128]).astype(bf16)
                bit = (row & 1).astype(f32)
                bit = jnp.broadcast_to(bit, (TL, 128)).astype(bf16)
                hi = ch * bit
                cx_ref[h, ip, pl.ds(0, TL), :] = ch - hi
                cx_ref[h, ip, pl.ds(TL, TL), :] = hi
        return 0

    lax.fori_loop(0, 8, body, 0)


def lookup(slot_ref, tab_ref, bins_ref, pos_ref):
    for r in range(16):
        tab_ref[pl.ds(r, 1), :] = slot_ref[pl.ds(128 * r, 128)].reshape(1, 128)
    p = tab_ref[...]
    core, x, y = (p >> 4) & 1, (p >> 2) & 3, p >> 9
    z, k = (p >> 5) & 15, p & 3
    tab = core * 1024 + x * 256 + y * 64 + z * 4 + k
    tt = jnp.concatenate([(tab & 255).astype(f32), (tab >> 8).astype(f32)], 0).astype(bf16)
    sub = lax.broadcasted_iota(jnp.int32, (128, 256), 0)
    s16 = lax.broadcasted_iota(jnp.int32, (16, 256), 0)

    def body(s, _):
        for u in range(8):
            t = 16 * s + 2 * u
            b = jnp.concatenate([bins_ref[pl.ds(t, 1), :], bins_ref[pl.ds(t + 1, 1), :]], 1)
            oh = jnp.where(sub == (b & 127), 1.0, 0.0).astype(bf16)
            v = jnp.dot(tt, oh, preferred_element_type=f32)
            full = v[:16] + 256.0 * v[16:]
            p = jnp.sum(jnp.where(s16 == (b >> 7), full, 0.0), axis=0, keepdims=True).astype(jnp.int32)
            pos_ref[pl.ds(t, 1), :] = p[:, :128]
            pos_ref[pl.ds(t + 1, 1), :] = p[:, 128:]
        return 0

    lax.fori_loop(0, 4, body, 0)


def pair_bins(mid_ref, off_ref, upper, s0, s1, ubin, vbin):
    s0[...] = jnp.zeros_like(s0)
    s1[...] = jnp.zeros_like(s1)
    s0[:, pl.ds(0, 64)] = (mid_ref[0] * NOFF + off_ref[0]).astype(f32)
    s1[pl.ds(0, 64), pl.ds(0, 64)] = (mid_ref[1] * NOFF + off_ref[1]).astype(f32)
    near, far = s0[...], s1[...]
    ubin[...] = jnp.where(upper, far[0:64], near).astype(jnp.int32)
    vbin[...] = pltpu.roll(jnp.where(upper, near, jnp.transpose(far)[0:64]), 64, 1).astype(jnp.int32)


def binning(pos_ref, cx_ref, acc_ref, base):
    sub = lax.broadcasted_iota(jnp.int32, (256, 128), 0).astype(f32).astype(bf16)
    one, zero = jnp.ones((), bf16), jnp.zeros((), bf16)

    def body(s, _):
        lhs, rhs = [], []
        for u in range(KB):
            t = KB * s + u
            for q in range(2):
                a = pos_ref[pl.ds(2 * t + q, 1), :] >> 1
                lo, hi = a & 255, a >> 8
                col = []
                for h in range(2):
                    key = jnp.where(hi == base + h, lo, -1).astype(f32)
                    key = jnp.broadcast_to(key, (256, 128)).astype(bf16)
                    col.append(jnp.where(sub == key, one, zero))
                lhs.append(jnp.concatenate(col, 0))
                rhs.append(cx_ref[q, t])
        o = lax.dot_general(jnp.concatenate(lhs, 1), jnp.concatenate(rhs, 1), (((1,), (1,)), ((), ())), preferred_element_type=f32)
        acc_ref[...] = acc_ref[...] + o
        return 0

    acc_ref[...] = jnp.zeros_like(acc_ref)
    lax.fori_loop(0, 32 // KB, body, 0)


KB = 4


def finish(total, fin, out_ref):
    for r in range(2):
        for h in range(2):
            fin[pl.ds(2 * r + h, 1), :] = total[r:r + 1, h * TL:h * TL + TL]
    t = fin[0:4, :]
    number = t[:, NL:NL + 1] + t[:, NL + 1:NL + 2]
    out_ref[...] = t[:, :NL] / jnp.sqrt(jnp.maximum(number, 1.0))


NX, NY, NZ = 4, 4, 16
MESH = pl.DeviceIdType.MESH


def place():
    blk = lax.axis_index("blk")
    return lax.axis_index("grp"), blk // (2 * NZ), lax.rem(blk // 2, NZ), lax.rem(blk, 2)


def device(x, y, z, core):
    return {"blk": (y * NZ + z) * 2 + core, "grp": x}


def plane_peer(d):
    x, y, z, core = place()
    return lax.rem(x + d // NY, NX), lax.rem(y + lax.rem(d, NY), NY), z, core


def line_peer(d):
    x, y, z, core = place()
    return x, y, lax.rem(z + d, NZ), core


def chip_neighbour(by, core):
    n = lax.axis_size("blk")
    chip = lax.axis_index("blk") // 2
    return {"blk": lax.rem(chip + by + n // 2, n // 2) * 2 + core, "grp": lax.axis_index("grp")}


def greet():
    barrier = pltpu.get_barrier_semaphore()
    x, y, z, core = place()

    def tell(device_id):
        pl.semaphore_signal(barrier, inc=1, device_id=device_id, device_id_type=MESH)

    tell(device(x, y, z, 1 - core))
    for by in (1, -1):
        for c in range(2):
            tell(chip_neighbour(by, c))

    def plane(d, _):
        tell(device(*plane_peer(d)))
        return 0

    def line(d, _):
        tell(device(*line_peer(d)))
        return 0

    lax.fori_loop(1, NX * NY, plane, 0)
    lax.fori_loop(1, NZ, line, 0)


def split_counts(v):
    lane = lax.rem(lax.broadcasted_iota(jnp.int32, v.shape, len(v.shape) - 1), TL)
    high = jnp.floor(v * (1.0 / 128.0)) * 128.0
    return jnp.where(lane == NL, high, jnp.where(lane == NL + 1, v - high, v))


def remote(src, dst, send, recv, to):
    return pltpu.make_async_remote_copy(
        src_ref=src, dst_ref=dst, send_sem=send, recv_sem=recv, device_id=to, device_id_type=MESH)


def kernel(x_ref, mid_ref, off_ref, slot_ref, kt_ref, out_ref,
           rows, tab, s0, s1, fin, bt, ag, ub, vb, w, ct, cx, ubin, vbin, vin, pos, away, came, keep,
           plane_out, plane_in, line_out, line_in,
           bin_sems, send1, send2, fwd_send, u_recv, v_recv,
           core_sems, plane_send, plane_recv, line_send, line_recv):
    greet()
    x, y, z, core = place()
    sibling = device(x, y, z, 1 - core)
    spread(x_ref, rows)
    for q in range(4):
        prep_tile(rows, bt, ag, q)
    pair_bins(mid_ref, off_ref, core == 1, s0, s1, ubin, vbin)
    pl.semaphore_wait(pltpu.get_barrier_semaphore(), NX * NY + NZ + 3)

    def bin_copy():
        return remote(vbin, vin, bin_sems.at[0], bin_sems.at[1], chip_neighbour(-1, 0))

    def up_copy(g):
        return remote(bt.at[g], ub.at[g], send1.at[g], u_recv.at[g], chip_neighbour(1, lax.rem(g, 2)))

    def side_copy(g):
        return remote(bt.at[g], vb.at[g], send1.at[g], v_recv.at[g], sibling)

    def down_copy(g):
        return remote(bt.at[g], vb.at[g], send2.at[g], v_recv.at[g], chip_neighbour(-1, 0))

    def forward(g):
        return remote(ub.at[g], ub.at[g], fwd_send.at[g], u_recv.at[g], sibling)

    @pl.when(core == 0)
    def _():
        bin_copy().start()

        def start(g, _):
            down_copy(g).start()
            side_copy(g).start()
            return 0

        lax.fori_loop(0, 8, start, 0)
        bin_copy().wait()

    @pl.when(core == 1)
    def _():
        def start(g, _):
            up_copy(g).start()
            return 0

        lax.fori_loop(0, 8, start, 0)
        vin[...] = vbin[...]

    ubin[...] = ubin[...] + vin[...]
    lookup(slot_ref, tab, ubin, pos)
    sign = jnp.where(core == 0, -1.0, 1.0)

    def chunk(s, _):
        first = 2 * (s // 2) + core
        g = jnp.where(lax.rem(s, 2) == 0, first, 4 * (s // 2) + 1 - first)
        forward(g).wait_recv()

        @pl.when(lax.rem(s, 2) == 0)
        def _():
            forward(g).start()

        side_copy(g).wait_recv()
        weights(ub, vb, w, g, sign)
        stage1(ag, w, ct, g)
        return 0

    lax.fori_loop(0, 8, chunk, 0)
    stage2(kt_ref, ct, pos, cx)

    binning(pos, cx, away, 2 * (1 - core))
    swap = remote(away, came, core_sems.at[0], core_sems.at[1], sibling)
    swap.start()
    binning(pos, cx, keep, 2 * core)
    swap.wait()

    def merge(d, _):
        at = pl.ds(pl.multiple_of(d * 32, 32), 32)
        v = split_counts(keep[at, :] + came[at, :])
        keep[at, :] = v
        plane_out[d] = v.astype(bf16)
        return 0

    lax.fori_loop(0, NX * NY, merge, 0)

    def plane_copy(d):
        px, py, pz, pc = plane_peer(d)
        return remote(plane_out.at[px * NY + py], plane_in.at[d], plane_send.at[d], plane_recv.at[d],
                      device(px, py, pz, pc))

    def start_plane(d, _):
        plane_copy(d).start()
        return 0

    lax.fori_loop(1, NX * NY, start_plane, 0)

    def take_plane(d, acc):
        plane_copy(d).wait()
        return acc + plane_in[d].astype(f32)

    mine = keep[pl.ds(pl.multiple_of((x * NY + y) * 32, 32), 32), :]
    total = lax.fori_loop(1, NX * NY, take_plane, mine)
    for i in range(NZ):
        line_out[i] = total[2 * i:2 * i + 2]

    def line_copy(d):
        px, py, pz, pc = line_peer(d)
        return remote(line_out.at[pz], line_in.at[d], line_send.at[d], line_recv.at[d], device(px, py, pz, pc))

    def start_line(d, _):
        line_copy(d).start()
        return 0

    lax.fori_loop(1, NZ, start_line, 0)

    def take_line(d, acc):
        line_copy(d).wait()
        return acc + line_in[d]

    finish(lax.fori_loop(1, NZ, take_line, line_out[z]), fin, out_ref)

    @pl.when(core == 0)
    def _():
        def drain(g, _):
            down_copy(g).wait_send()
            side_copy(g).wait_send()
            return 0

        lax.fori_loop(0, 8, drain, 0)

    @pl.when(core == 1)
    def _():
        def drain(g, _):
            up_copy(g).wait_send()
            return 0

        lax.fori_loop(0, 8, drain, 0)

    def drain(s, _):
        forward(2 * s + core).wait_send()
        return 0

    lax.fori_loop(0, 4, drain, 0)


def run(*args):
    vm = pltpu.VMEM
    dma = pltpu.SemaphoreType.DMA
    i32 = jnp.int32
    return pl.pallas_call(
        kernel, out_shape=jax.ShapeDtypeStruct((4, NL), f32),
        in_specs=[pl.BlockSpec(memory_space=pltpu.VMEM)] * 5,
        out_specs=pl.BlockSpec(memory_space=pltpu.VMEM),
        scratch_shapes=[
            vm((8, 512, 128), f32), vm((16, 128), i32), vm((64, 128), f32), vm((128, 128), f32), vm((8, 128), f32),
            vm((8, 256, 128), bf16), vm((32, 64, 128), f32), vm((8, 256, 128), bf16), vm((8, 256, 128), bf16),
            vm((2, 2, 256, 128), bf16), vm((2, 32, 1024, 128), bf16), vm((2, 32, 256, 128), bf16),
            vm((64, 128), i32), vm((64, 128), i32), vm((64, 128), i32), vm((64, 128), i32),
            vm((512, 256), f32), vm((512, 256), f32), vm((512, 256), f32),
            vm((16, 32, 256), bf16), vm((16, 32, 256), bf16), vm((16, 2, 256), f32), vm((16, 2, 256), f32),
            dma((2,)), dma((8,)), dma((8,)), dma((8,)), dma((8,)), dma((8,)),
            dma((2,)), dma((16,)), dma((16,)), dma((16,)), dma((16,)),
        ],
        compiler_params=pltpu.CompilerParams(
            vmem_limit_bytes=60 * 2**20, collective_id=0, has_side_effects=True),
    )(*args)


def shards(spectra, mid_bin, off_bin, owner_slot):
    return run(spectra, mid_bin, off_bin, owner_slot, lag_matrix()).T


def solution(mesh):
    in_specs = (
        P(("blk", "grp"), None, None),
        P(None, ("blk", "grp"), None),
        P(None, ("blk", "grp"), None),
        P(),
    )
    return jax.shard_map(shards, mesh=mesh, in_specs=in_specs, out_specs=P(None, ("blk", "grp")), check_vma=False)
```

```python
import jax
import jax.numpy as jnp
import numpy as np
from jax import lax
from jax.experimental import pallas as pl
from jax.experimental.pallas import tpu as pltpu
from jax.sharding import PartitionSpec as P

LAG = 50
NOFF = 16
F = 501
W = 4
FP = 512
TL = 128
NL = 2 * LAG + 1
bf16, f32 = jnp.bfloat16, jnp.float32


def lag_matrix():
    freq = np.arange(F, dtype=np.float32)
    lags = (np.arange(NL) - LAG).astype(np.float32)
    angle = (np.float32(2.0 * np.pi) * freq[:, None] * lags[None, :] / np.float32(2 * (F - 1))).astype(np.float32)
    w = np.where((freq == 0) | (freq == F - 1), 1.0, 2.0).astype(np.float32) / np.sqrt(np.float32(W * F))
    k = np.zeros((TL, 2 * FP), np.float32)
    k[:NL, :F] = (w[:, None] * np.cos(angle)).T
    k[:NL, FP:FP + F] = (-w[:, None] * np.sin(angle)).T
    return jnp.asarray(k, bf16)


def spread(x_ref, rows_ref):
    for i in range(64):
        x = x_ref[i].astype(f32)
        for t in range(8):
            n = min(128, 2 * F - 128 * t)
            rows_ref[t, pl.ds(8 * i, W), pl.ds(0, n)] = x[:, 128 * t:128 * t + n]


def parts(rows_ref, q):
    lane = lax.broadcasted_iota(jnp.int32, (64, 128), 1)
    cut = F - FP + 128
    gap = FP - F
    out = []
    for w in range(W):
        def tile(t):
            return rows_ref[t, pl.ds(w, 64, stride=8), :]

        re = tile(q)
        im = jnp.where(lane < gap, pltpu.roll(tile(q + 3), gap, 1), pltpu.roll(tile(q + 4), gap, 1))
        if q == 3:
            re, im = jnp.where(lane < cut, re, 0.0), jnp.where(lane < cut, im, 0.0)
        out += [re, im]
    return out


def prep_tile(rows_ref, bt_ref, ag_ref, q):
    lane = lax.broadcasted_iota(jnp.int32, (64, 128), 1)
    xs = parts(rows_ref, q)
    for k in range(8):
        x = xs[k]
        y = jnp.transpose(jnp.concatenate([x, pltpu.roll(x, 96, 1)], 0)).astype(bf16)
        bt_ref[2 * q, pl.ds(k * 32, 32), :] = y[0:32]
        bt_ref[2 * q + 1, pl.ds(k * 32, 32), :] = y[64:96]
    for s in range(4):
        for h in range(2):
            acc = None
            for m in range(4):
                shift = (32 * (m - s)) % 128
                v = xs[4 * h + m]
                v = pltpu.roll(v, shift, 1) if shift else v
                acc = v if acc is None else jnp.where(lane >= 32 * m, v, acc)
            ag_ref[(4 * q + s) * 2 + h] = acc


def weights(u_ref, v_ref, w_ref, gp, sign):
    lane = lax.broadcasted_iota(jnp.int32, (32, 128), 1)
    left = lane < 64
    sgn = jnp.where(left, 1.0, sign)
    for k in range(8):
        u = u_ref[gp, pl.ds(k * 32, 32), :].astype(f32)
        v = v_ref[gp, pl.ds(k * 32, 32), :].astype(f32)
        ur, vr = pltpu.roll(u, 64, 1), pltpu.roll(v, 64, 1)
        for n, val in ((0, jnp.where(left, u, vr)), (1, jnp.where(left, ur, v))):
            w_ref[n, 0, pl.ds(k * 32, 32), :] = val.astype(bf16)
            other = val * sgn if k % 2 == 0 else -(val * sgn)
            w_ref[n, 1, pl.ds((k ^ 1) * 32, 32), :] = other.astype(bf16)


def stage1(ag_ref, w_ref, ct_ref, gp):
    MI = 16
    row = lax.broadcasted_iota(jnp.int32, (32, 128), 0)
    lane = lax.broadcasted_iota(jnp.int32, (32, 128), 1)
    mask = jnp.where((lane & 31) == row, 1.0, 0.0).astype(bf16)

    def body(ib, _):
        for n in range(2):
            w = jnp.concatenate([w_ref[n, 0], w_ref[n, 1]], 1)
            for h in range(MH):
                parts = []
                for ii in range(MI):
                    halves = []
                    for q in range(2):
                        a = ag_ref[(2 * gp + n) * 2 + q, pl.ds((ib * MH + h) * MI + ii, 1), :]
                        a = jnp.broadcast_to(a, (16, 128)).astype(bf16)
                        halves.append(jnp.concatenate([a, a], 0) * mask)
                    parts.append(jnp.concatenate(halves, 1))
                e = jnp.concatenate(parts, 0)
                o = jnp.dot(e, w, preferred_element_type=f32).astype(bf16)
                r0 = pl.multiple_of((2 * gp + n) * 32, 32)
                for ii in range(MI):
                    p = ((ib * MH + h) * MI + ii) // 2
                    ct_ref[ii % 2, p, pl.ds(r0, 32), :] = o[ii * 32:ii * 32 + 32, 0:128]
                    ct_ref[ii % 2, p, pl.ds(r0 + FP, 32), :] = o[ii * 32:ii * 32 + 32, 128:256]
        return 0

    lax.fori_loop(0, 64 // (MI * MH), body, 0)


MH = 4


def stage2(kt_ref, ct_ref, pos_ref, cx_ref):
    sub = lax.broadcasted_iota(jnp.int32, (TL, 128), 0)
    count = (sub == NL) | (sub == NL + 1)

    def body(s, _):
        for u in range(8):
            ip = 8 * s + u
            w = jnp.concatenate([ct_ref[0, ip], ct_ref[1, ip]], 1)
            c = jnp.dot(kt_ref[...], w, preferred_element_type=f32)
            for h in range(2):
                row = pos_ref[pl.ds(2 * ip + h, 1), :]
                ch = jnp.where(count, 1.0, c[:, h * 128:h * 128 + 128]).astype(bf16)
                bit = (row & 1).astype(f32)
                bit = jnp.broadcast_to(bit, (TL, 128)).astype(bf16)
                hi = ch * bit
                cx_ref[h, ip, pl.ds(0, TL), :] = ch - hi
                cx_ref[h, ip, pl.ds(TL, TL), :] = hi
        return 0

    lax.fori_loop(0, 4, body, 0)


def lookup(slot_ref, tab_ref, bins_ref, pos_ref):
    for r in range(16):
        tab_ref[pl.ds(r, 1), :] = slot_ref[pl.ds(128 * r, 128)].reshape(1, 128)
    p = tab_ref[...]
    core, x, y = (p >> 4) & 1, (p >> 2) & 3, p >> 9
    z, k = (p >> 5) & 15, p & 3
    tab = core * 1024 + x * 256 + y * 64 + z * 4 + k
    tt = jnp.concatenate([(tab & 255).astype(f32), (tab >> 8).astype(f32)], 0).astype(bf16)
    sub = lax.broadcasted_iota(jnp.int32, (128, 256), 0)
    s16 = lax.broadcasted_iota(jnp.int32, (16, 256), 0)

    def body(s, _):
        for u in range(8):
            t = 16 * s + 2 * u
            b = jnp.concatenate([bins_ref[pl.ds(t, 1), :], bins_ref[pl.ds(t + 1, 1), :]], 1)
            oh = jnp.where(sub == (b & 127), 1.0, 0.0).astype(bf16)
            v = jnp.dot(tt, oh, preferred_element_type=f32)
            full = v[:16] + 256.0 * v[16:]
            p = jnp.sum(jnp.where(s16 == (b >> 7), full, 0.0), axis=0, keepdims=True).astype(jnp.int32)
            pos_ref[pl.ds(t, 1), :] = p[:, :128]
            pos_ref[pl.ds(t + 1, 1), :] = p[:, 128:]
        return 0

    lax.fori_loop(0, 4, body, 0)


def pair_bins(mid_ref, off_ref, upper, s0, s1, ubin, vbin):
    s0[...] = jnp.zeros_like(s0)
    s1[...] = jnp.zeros_like(s1)
    s0[:, pl.ds(0, 64)] = (mid_ref[0] * NOFF + off_ref[0]).astype(f32)
    s1[pl.ds(0, 64), pl.ds(0, 64)] = (mid_ref[1] * NOFF + off_ref[1]).astype(f32)
    near, far = s0[...], s1[...]
    ubin[...] = jnp.where(upper, far[0:64], near).astype(jnp.int32)
    vbin[...] = pltpu.roll(jnp.where(upper, near, jnp.transpose(far)[0:64]), 64, 1).astype(jnp.int32)


def binning(pos_ref, cx_ref, acc_ref, base):
    n = acc_ref.shape[0] // 256
    sub = lax.broadcasted_iota(jnp.int32, (256, 128), 0).astype(f32).astype(bf16)
    one, zero = jnp.ones((), bf16), jnp.zeros((), bf16)

    def body(s, _):
        lhs, rhs = [], []
        for u in range(KB):
            t = KB * s + u
            for q in range(2):
                a = pos_ref[pl.ds(2 * t + q, 1), :] >> 1
                lo, hi = a & 255, a >> 8
                col = []
                for h in range(n):
                    key = jnp.where(hi == base + h, lo, -1).astype(f32)
                    key = jnp.broadcast_to(key, (256, 128)).astype(bf16)
                    col.append(jnp.where(sub == key, one, zero))
                lhs.append(jnp.concatenate(col, 0))
                rhs.append(cx_ref[q, t])
        o = lax.dot_general(jnp.concatenate(lhs, 1), jnp.concatenate(rhs, 1), (((1,), (1,)), ((), ())), preferred_element_type=f32)
        acc_ref[...] = acc_ref[...] + o
        return 0

    acc_ref[...] = jnp.zeros_like(acc_ref)
    lax.fori_loop(0, 32 // KB, body, 0)


KB = 16


def finish(total, out_ref):
    for r in range(2):
        for h in range(2):
            out_ref[pl.ds(2 * r + h, 1), :] = total[r:r + 1, h * TL:h * TL + TL]
    t = out_ref[...]
    number = t[:, NL:NL + 1] + t[:, NL + 1:NL + 2]
    out_ref[...] = t / jnp.sqrt(jnp.maximum(number, 1.0))


NX, NY, NZ = 4, 4, 16
MESH = pl.DeviceIdType.MESH


def place():
    blk = lax.axis_index("blk")
    return lax.axis_index("grp"), blk // (2 * NZ), lax.rem(blk // 2, NZ), lax.rem(blk, 2)


def device(x, y, z, core):
    return {"blk": (y * NZ + z) * 2 + core, "grp": x}


def plane_peer(d):
    x, y, z, core = place()
    return lax.rem(x + d // NY, NX), lax.rem(y + lax.rem(d, NY), NY), z, core


def line_peer(d):
    x, y, z, core = place()
    return x, y, lax.rem(z + d, NZ), core


def chip_neighbour(by, core):
    n = lax.axis_size("blk")
    chip = lax.axis_index("blk") // 2
    return {"blk": lax.rem(chip + by + n // 2, n // 2) * 2 + core, "grp": lax.axis_index("grp")}


def greet():
    barrier = pltpu.get_barrier_semaphore()
    x, y, z, core = place()

    def tell(device_id):
        pl.semaphore_signal(barrier, inc=1, device_id=device_id, device_id_type=MESH)

    tell(device(x, y, z, 1 - core))
    for by in (1, -1):
        for c in range(2):
            tell(chip_neighbour(by, c))

    def plane(d, _):
        tell(device(*plane_peer(d)))
        return 0

    def line(d, _):
        tell(device(*line_peer(d)))
        return 0

    lax.fori_loop(1, NX * NY, plane, 0)
    lax.fori_loop(1, NZ, line, 0)


def split_counts(v):
    lane = lax.rem(lax.broadcasted_iota(jnp.int32, v.shape, len(v.shape) - 1), TL)
    high = jnp.floor(v * (1.0 / 128.0)) * 128.0
    return jnp.where(lane == NL, high, jnp.where(lane == NL + 1, v - high, v))


def remote(src, dst, send, recv, to):
    return pltpu.make_async_remote_copy(
        src_ref=src, dst_ref=dst, send_sem=send, recv_sem=recv, device_id=to, device_id_type=MESH)


def hops(d, size):
    return min(d, size - d)


def kernel(x_ref, mid_ref, off_ref, slot_ref, kt_ref, out_ref,
           rows, tab, s0, s1, bt, ag, ub, vb, w, ct, cx, ubin, vbin, vin, pos, away, came, keep,
           plane_out, plane_in, line_out, line_in,
           bin_sems, send1, send2, fwd_send, u_recv, v_recv,
           core_sems, plane_send, plane_recv, line_send, line_recv):
    greet()
    x, y, z, core = place()
    sibling = device(x, y, z, 1 - core)
    spread(x_ref, rows)
    for q in range(4):
        prep_tile(rows, bt, ag, q)
    pair_bins(mid_ref, off_ref, core == 1, s0, s1, ubin, vbin)
    pl.semaphore_wait(pltpu.get_barrier_semaphore(), NX * NY + NZ + 3)

    def bin_copy():
        return remote(vbin, vin, bin_sems.at[0], bin_sems.at[1], chip_neighbour(-1, 0))

    def up_copy(g):
        return remote(bt.at[g], ub.at[g], send1.at[g], u_recv.at[g], chip_neighbour(1, lax.rem(g, 2)))

    def side_copy(g):
        return remote(bt.at[g], vb.at[g], send1.at[g], v_recv.at[g], sibling)

    def down_copy(g):
        return remote(bt.at[g], vb.at[g], send2.at[g], v_recv.at[g], chip_neighbour(-1, 0))

    def forward(g):
        return remote(ub.at[g], ub.at[g], fwd_send.at[g], u_recv.at[g], sibling)

    @pl.when(core == 0)
    def _():
        bin_copy().start()

        def start(g, _):
            down_copy(g).start()
            side_copy(g).start()
            return 0

        lax.fori_loop(0, 8, start, 0)
        bin_copy().wait()

    @pl.when(core == 1)
    def _():
        def start(g, _):
            up_copy(g).start()
            return 0

        lax.fori_loop(0, 8, start, 0)
        vin[...] = vbin[...]

    ubin[...] = ubin[...] + vin[...]
    lookup(slot_ref, tab, ubin, pos)
    sign = jnp.where(core == 0, -1.0, 1.0)

    def chunk(s, _):
        first = 2 * (s // 2) + core
        g = jnp.where(lax.rem(s, 2) == 0, first, 4 * (s // 2) + 1 - first)
        forward(g).wait_recv()

        @pl.when(lax.rem(s, 2) == 0)
        def _():
            forward(g).start()

        side_copy(g).wait_recv()
        weights(ub, vb, w, g, sign)
        stage1(ag, w, ct, g)
        return 0

    lax.fori_loop(0, 8, chunk, 0)
    stage2(kt_ref, ct, pos, cx)

    binning(pos, cx, away, 2 * (1 - core))
    swap = remote(away, came, core_sems.at[0], core_sems.at[1], sibling)
    swap.start()

    def plane_copy(d):
        px, py, pz, pc = plane_peer(d)
        return remote(plane_out.at[px * NY + py], plane_in.at[d], plane_send.at[d], plane_recv.at[d],
                      device(px, py, pz, pc))

    def merge(d, _):
        at = pl.ds(pl.multiple_of(d * 32, 32), 32)
        v = split_counts(keep[at, :] + came[at, :])
        keep[at, :] = v
        plane_out[d] = v.astype(bf16)
        return 0

    far_first = sorted(range(1, NX * NY), key=lambda d: -hops(d // NY, NX) - hops(d % NY, NY))
    for piece in range(2):
        binning(pos, cx, keep.at[pl.ds(256 * piece, 256)], 2 * core + piece)
        if piece == 0:
            swap.wait()
        lax.fori_loop(8 * piece, 8 * piece + 8, merge, 0)
        for d in far_first:
            @pl.when(plane_peer(d)[0] // 2 == piece)
            def _():
                plane_copy(d).start()

    def take_plane(d, acc):
        plane_copy(d).wait()
        return acc + plane_in[d].astype(f32)

    mine = keep[pl.ds(pl.multiple_of((x * NY + y) * 32, 32), 32), :]
    total = lax.fori_loop(1, NX * NY, take_plane, mine)
    for i in range(NZ):
        line_out[i] = total[2 * i:2 * i + 2]

    def line_copy(d):
        px, py, pz, pc = line_peer(d)
        return remote(line_out.at[pz], line_in.at[d], line_send.at[d], line_recv.at[d], device(px, py, pz, pc))

    for d in sorted(range(1, NZ), key=lambda d: -hops(d, NZ)):
        line_copy(d).start()

    def take_line(d, acc):
        line_copy(d).wait()
        return acc + line_in[d]

    finish(lax.fori_loop(1, NZ, take_line, line_out[z]), out_ref)

    @pl.when(core == 0)
    def _():
        def drain(g, _):
            down_copy(g).wait_send()
            side_copy(g).wait_send()
            return 0

        lax.fori_loop(0, 8, drain, 0)

    @pl.when(core == 1)
    def _():
        def drain(g, _):
            up_copy(g).wait_send()
            return 0

        lax.fori_loop(0, 8, drain, 0)

    def drain(s, _):
        forward(2 * s + core).wait_send()
        return 0

    lax.fori_loop(0, 4, drain, 0)


def run(*args):
    vm = pltpu.VMEM
    dma = pltpu.SemaphoreType.DMA
    i32 = jnp.int32
    return pl.pallas_call(
        kernel, out_shape=jax.ShapeDtypeStruct((4, TL), f32),
        in_specs=[pl.BlockSpec(memory_space=pltpu.VMEM)] * 5,
        out_specs=pl.BlockSpec(memory_space=pltpu.VMEM),
        scratch_shapes=[
            vm((8, 512, 128), f32), vm((16, 128), i32), vm((64, 128), f32), vm((128, 128), f32),
            vm((8, 256, 128), bf16), vm((32, 64, 128), f32), vm((8, 256, 128), bf16), vm((8, 256, 128), bf16),
            vm((2, 2, 256, 128), bf16), vm((2, 32, 1024, 128), bf16), vm((2, 32, 256, 128), bf16),
            vm((64, 128), i32), vm((64, 128), i32), vm((64, 128), i32), vm((64, 128), i32),
            vm((512, 256), f32), vm((512, 256), f32), vm((512, 256), f32),
            vm((16, 32, 256), bf16), vm((16, 32, 256), bf16), vm((16, 2, 256), f32), vm((16, 2, 256), f32),
            dma((2,)), dma((8,)), dma((8,)), dma((8,)), dma((8,)), dma((8,)),
            dma((2,)), dma((16,)), dma((16,)), dma((16,)), dma((16,)),
        ],
        compiler_params=pltpu.CompilerParams(
            vmem_limit_bytes=60 * 2**20, collective_id=0, has_side_effects=True),
    )(*args)


def shards(spectra, mid_bin, off_bin, owner_slot):
    return run(spectra, mid_bin, off_bin, owner_slot, lag_matrix())[:, :NL].T


def solution(mesh):
    in_specs = (
        P(("blk", "grp"), None, None),
        P(None, ("blk", "grp"), None),
        P(None, ("blk", "grp"), None),
        P(),
    )
    return jax.shard_map(shards, mesh=mesh, in_specs=in_specs, out_specs=P(None, ("blk", "grp")), check_vma=False)
```

```python
import jax
import jax.numpy as jnp
import numpy as np
from jax import lax
from jax.experimental import pallas as pl
from jax.experimental.pallas import tpu as pltpu
from jax.sharding import PartitionSpec as P

LAG = 50
NOFF = 16
F = 501
W = 4
FP = 512
TL = 128
NL = 2 * LAG + 1
bf16, f32 = jnp.bfloat16, jnp.float32


def lag_matrix():
    freq = np.arange(F, dtype=np.float32)
    lags = (np.arange(NL) - LAG).astype(np.float32)
    angle = (np.float32(2.0 * np.pi) * freq[:, None] * lags[None, :] / np.float32(2 * (F - 1))).astype(np.float32)
    w = np.where((freq == 0) | (freq == F - 1), 1.0, 2.0).astype(np.float32) / np.sqrt(np.float32(W * F))
    k = np.zeros((TL, 2 * FP), np.float32)
    k[:NL, :F] = (w[:, None] * np.cos(angle)).T
    k[:NL, FP:FP + F] = (-w[:, None] * np.sin(angle)).T
    return jnp.asarray(k, bf16)


def spread(x_ref, rows_ref):
    for i in range(64):
        x = x_ref[i].astype(f32)
        for t in range(8):
            n = min(128, 2 * F - 128 * t)
            rows_ref[t, pl.ds(8 * i, W), pl.ds(0, n)] = x[:, 128 * t:128 * t + n]


def parts(rows_ref, q):
    lane = lax.broadcasted_iota(jnp.int32, (64, 128), 1)
    cut = F - FP + 128
    gap = FP - F
    out = []
    for w in range(W):
        def tile(t):
            return rows_ref[t, pl.ds(w, 64, stride=8), :]

        re = tile(q)
        im = jnp.where(lane < gap, pltpu.roll(tile(q + 3), gap, 1), pltpu.roll(tile(q + 4), gap, 1))
        if q == 3:
            re, im = jnp.where(lane < cut, re, 0.0), jnp.where(lane < cut, im, 0.0)
        out += [re, im]
    return out


def prep_tile(rows_ref, bt_ref, ag_ref, q):
    lane = lax.broadcasted_iota(jnp.int32, (64, 128), 1)
    xs = parts(rows_ref, q)
    for k in range(8):
        x = xs[k]
        y = jnp.transpose(jnp.concatenate([x, pltpu.roll(x, 96, 1)], 0)).astype(bf16)
        bt_ref[2 * q, pl.ds(k * 32, 32), :] = y[0:32]
        bt_ref[2 * q + 1, pl.ds(k * 32, 32), :] = y[64:96]
    for s in range(4):
        for h in range(2):
            acc = None
            for m in range(4):
                shift = (32 * (m - s)) % 128
                v = xs[4 * h + m]
                v = pltpu.roll(v, shift, 1) if shift else v
                acc = v if acc is None else jnp.where(lane >= 32 * m, v, acc)
            ag_ref[(4 * q + s) * 2 + h] = acc


def weights(u_ref, v_ref, w_ref, gp, sign):
    lane = lax.broadcasted_iota(jnp.int32, (32, 128), 1)
    left = lane < 64
    sgn = jnp.where(left, 1.0, sign)
    for k in range(8):
        u = u_ref[gp, pl.ds(k * 32, 32), :].astype(f32)
        v = v_ref[gp, pl.ds(k * 32, 32), :].astype(f32)
        ur, vr = pltpu.roll(u, 64, 1), pltpu.roll(v, 64, 1)
        for n, val in ((0, jnp.where(left, u, vr)), (1, jnp.where(left, ur, v))):
            w_ref[n, 0, pl.ds(k * 32, 32), :] = val.astype(bf16)
            other = val * sgn if k % 2 == 0 else -(val * sgn)
            w_ref[n, 1, pl.ds((k ^ 1) * 32, 32), :] = other.astype(bf16)


def stage1(ag_ref, w_ref, ct_ref, gp):
    MI = 16
    row = lax.broadcasted_iota(jnp.int32, (32, 128), 0)
    lane = lax.broadcasted_iota(jnp.int32, (32, 128), 1)
    mask = jnp.where((lane & 31) == row, 1.0, 0.0).astype(bf16)

    def body(ib, _):
        for n in range(2):
            w = jnp.concatenate([w_ref[n, 0], w_ref[n, 1]], 1)
            for h in range(MH):
                parts = []
                for ii in range(MI):
                    halves = []
                    for q in range(2):
                        a = ag_ref[(2 * gp + n) * 2 + q, pl.ds((ib * MH + h) * MI + ii, 1), :]
                        a = jnp.broadcast_to(a, (16, 128)).astype(bf16)
                        halves.append(jnp.concatenate([a, a], 0) * mask)
                    parts.append(jnp.concatenate(halves, 1))
                e = jnp.concatenate(parts, 0)
                o = jnp.dot(e, w, preferred_element_type=f32).astype(bf16)
                r0 = pl.multiple_of((2 * gp + n) * 32, 32)
                for ii in range(MI):
                    p = ((ib * MH + h) * MI + ii) // 2
                    ct_ref[ii % 2, p, pl.ds(r0, 32), :] = o[ii * 32:ii * 32 + 32, 0:128]
                    ct_ref[ii % 2, p, pl.ds(r0 + FP, 32), :] = o[ii * 32:ii * 32 + 32, 128:256]
        return 0

    lax.fori_loop(0, 64 // (MI * MH), body, 0)


MH = 4


def stage2(kt_ref, ct_ref, pos_ref, cx_ref):
    sub = lax.broadcasted_iota(jnp.int32, (TL, 128), 0)
    count = (sub == NL) | (sub == NL + 1)

    def body(s, _):
        for u in range(8):
            ip = 8 * s + u
            w = jnp.concatenate([ct_ref[0, ip], ct_ref[1, ip]], 1)
            c = jnp.dot(kt_ref[...], w, preferred_element_type=f32)
            for h in range(2):
                row = pos_ref[pl.ds(2 * ip + h, 1), :]
                ch = jnp.where(count, 1.0, c[:, h * 128:h * 128 + 128]).astype(bf16)
                bit = (row & 1).astype(f32)
                bit = jnp.broadcast_to(bit, (TL, 128)).astype(bf16)
                hi = ch * bit
                cx_ref[h, ip, pl.ds(0, TL), :] = ch - hi
                cx_ref[h, ip, pl.ds(TL, TL), :] = hi
        return 0

    lax.fori_loop(0, 4, body, 0)


def lookup(slot_ref, tab_ref, bins_ref, pos_ref):
    for r in range(16):
        tab_ref[pl.ds(r, 1), :] = slot_ref[pl.ds(128 * r, 128)].reshape(1, 128)
    p = tab_ref[...]
    core, x, y = (p >> 4) & 1, (p >> 2) & 3, p >> 9
    z, k = (p >> 5) & 15, p & 3
    tab = core * 1024 + x * 256 + y * 64 + z * 4 + k
    tt = jnp.concatenate([(tab & 255).astype(f32), (tab >> 8).astype(f32)], 0).astype(bf16)
    sub = lax.broadcasted_iota(jnp.int32, (128, 256), 0)
    s16 = lax.broadcasted_iota(jnp.int32, (16, 256), 0)

    def body(s, _):
        for u in range(8):
            t = 16 * s + 2 * u
            b = jnp.concatenate([bins_ref[pl.ds(t, 1), :], bins_ref[pl.ds(t + 1, 1), :]], 1)
            oh = jnp.where(sub == (b & 127), 1.0, 0.0).astype(bf16)
            v = jnp.dot(tt, oh, preferred_element_type=f32)
            full = v[:16] + 256.0 * v[16:]
            p = jnp.sum(jnp.where(s16 == (b >> 7), full, 0.0), axis=0, keepdims=True).astype(jnp.int32)
            pos_ref[pl.ds(t, 1), :] = p[:, :128]
            pos_ref[pl.ds(t + 1, 1), :] = p[:, 128:]
        return 0

    lax.fori_loop(0, 4, body, 0)


def pair_bins(mid_ref, off_ref, upper, s0, s1, ubin, vbin):
    s0[...] = jnp.zeros_like(s0)
    s1[...] = jnp.zeros_like(s1)
    s0[:, pl.ds(0, 64)] = (mid_ref[0] * NOFF + off_ref[0]).astype(f32)
    s1[pl.ds(0, 64), pl.ds(0, 64)] = (mid_ref[1] * NOFF + off_ref[1]).astype(f32)
    near, far = s0[...], s1[...]
    ubin[...] = jnp.where(upper, far[0:64], near).astype(jnp.int32)
    vbin[...] = pltpu.roll(jnp.where(upper, near, jnp.transpose(far)[0:64]), 64, 1).astype(jnp.int32)


def binning(pos_ref, cx_ref, acc_ref, base):
    n = acc_ref.shape[0] // 256
    sub = lax.broadcasted_iota(jnp.int32, (256, 128), 0).astype(f32).astype(bf16)
    one, zero = jnp.ones((), bf16), jnp.zeros((), bf16)

    def body(s, _):
        lhs, rhs = [], []
        for u in range(KB):
            t = KB * s + u
            for q in range(2):
                a = pos_ref[pl.ds(2 * t + q, 1), :] >> 1
                lo, hi = a & 255, a >> 8
                col = []
                for h in range(n):
                    key = jnp.where(hi == base + h, lo, -1).astype(f32)
                    key = jnp.broadcast_to(key, (256, 128)).astype(bf16)
                    col.append(jnp.where(sub == key, one, zero))
                lhs.append(jnp.concatenate(col, 0))
                rhs.append(cx_ref[q, t])
        o = lax.dot_general(jnp.concatenate(lhs, 1), jnp.concatenate(rhs, 1), (((1,), (1,)), ((), ())), preferred_element_type=f32)
        acc_ref[...] = acc_ref[...] + o
        return 0

    acc_ref[...] = jnp.zeros_like(acc_ref)
    lax.fori_loop(0, 32 // KB, body, 0)


KB = 16


def finish(total, out_ref):
    for r in range(2):
        for h in range(2):
            out_ref[pl.ds(2 * r + h, 1), :] = total[r:r + 1, h * TL:h * TL + TL]
    t = out_ref[...]
    number = t[:, NL:NL + 1] + t[:, NL + 1:NL + 2]
    out_ref[...] = t / jnp.sqrt(jnp.maximum(number, 1.0))


NX, NY, NZ = 4, 4, 16
MESH = pl.DeviceIdType.MESH


def place():
    blk = lax.axis_index("blk")
    return lax.axis_index("grp"), blk // (2 * NZ), lax.rem(blk // 2, NZ), lax.rem(blk, 2)


def device(x, y, z, core):
    return {"blk": (y * NZ + z) * 2 + core, "grp": x}


def plane_peer(d):
    x, y, z, core = place()
    return lax.rem(x + d // NY, NX), lax.rem(y + lax.rem(d, NY), NY), z, core


def line_peer(d):
    x, y, z, core = place()
    return x, y, lax.rem(z + d, NZ), core


def chip_neighbour(by, core):
    n = lax.axis_size("blk")
    chip = lax.axis_index("blk") // 2
    return {"blk": lax.rem(chip + by + n // 2, n // 2) * 2 + core, "grp": lax.axis_index("grp")}


def torus_neighbours():
    x, y, z, core = place()
    for by in (1, -1):
        yield device(lax.rem(x + by + NX, NX), y, z, core)
        yield device(x, lax.rem(y + by + NY, NY), z, core)
        yield device(x, y, lax.rem(z + by + NZ, NZ), core)


def greet():
    barrier = pltpu.get_barrier_semaphore()
    x, y, z, core = place()
    near = [device(x, y, z, 1 - core)]
    near += [chip_neighbour(by, c) for by in (1, -1) for c in range(2)]
    near += list(torus_neighbours())
    for device_id in near:
        pl.semaphore_signal(barrier, inc=1, device_id=device_id, device_id_type=MESH)
    return len(near)


def split_counts(v):
    lane = lax.rem(lax.broadcasted_iota(jnp.int32, v.shape, len(v.shape) - 1), TL)
    high = jnp.floor(v * (1.0 / 128.0)) * 128.0
    return jnp.where(lane == NL, high, jnp.where(lane == NL + 1, v - high, v))


def remote(src, dst, send, recv, to):
    return pltpu.make_async_remote_copy(
        src_ref=src, dst_ref=dst, send_sem=send, recv_sem=recv, device_id=to, device_id_type=MESH)


def hops(d, size):
    return min(d, size - d)


def kernel(x_ref, mid_ref, off_ref, slot_ref, kt_ref, out_ref,
           rows, tab, s0, s1, bt, ag, ub, vb, w, ct, cx, ubin, vbin, vin, pos, away, came, keep,
           plane_out, plane_in, line_out, line_in,
           bin_sems, send1, send2, fwd_send, u_recv, v_recv,
           rounds, core_sems, plane_send, plane_recv, line_send, line_recv):
    near = greet()
    x, y, z, core = place()
    sibling = device(x, y, z, 1 - core)
    spread(x_ref, rows)
    prep_tile(rows, bt, ag, 0)
    pair_bins(mid_ref, off_ref, core == 1, s0, s1, ubin, vbin)
    pl.semaphore_wait(pltpu.get_barrier_semaphore(), near)

    def bin_copy():
        return remote(vbin, vin, bin_sems.at[0], bin_sems.at[1], chip_neighbour(-1, 0))

    def up_copy(g):
        return remote(bt.at[g], ub.at[g], send1.at[g], u_recv.at[g], chip_neighbour(1, lax.rem(g, 2)))

    def side_copy(g):
        return remote(bt.at[g], vb.at[g], send1.at[g], v_recv.at[g], sibling)

    def down_copy(g):
        return remote(bt.at[g], vb.at[g], send2.at[g], v_recv.at[g], chip_neighbour(-1, 0))

    def forward(g):
        return remote(ub.at[g], ub.at[g], fwd_send.at[g], u_recv.at[g], sibling)

    @pl.when(core == 0)
    def _():
        bin_copy().start()

    for q in range(4):
        if q > 0:
            prep_tile(rows, bt, ag, q)

        @pl.when(core == 0)
        def _():
            for g in (2 * q, 2 * q + 1):
                down_copy(g).start()
                side_copy(g).start()

        @pl.when(core == 1)
        def _():
            for g in (2 * q, 2 * q + 1):
                up_copy(g).start()

    @pl.when(core == 0)
    def _():
        bin_copy().wait()

    @pl.when(core == 1)
    def _():
        vin[...] = vbin[...]

    ubin[...] = ubin[...] + vin[...]
    lookup(slot_ref, tab, ubin, pos)
    sign = jnp.where(core == 0, -1.0, 1.0)

    def chunk(s, _):
        first = 2 * (s // 2) + core
        g = jnp.where(lax.rem(s, 2) == 0, first, 4 * (s // 2) + 1 - first)
        forward(g).wait_recv()

        @pl.when(lax.rem(s, 2) == 0)
        def _():
            forward(g).start()

        side_copy(g).wait_recv()
        weights(ub, vb, w, g, sign)
        stage1(ag, w, ct, g)

        @pl.when(lax.rem(s, 3) == 2)
        def _():
            hear(s // 3)
            spread_word(s // 3 + 1)

        return 0

    def spread_word(r):
        for device_id in torus_neighbours():
            pl.semaphore_signal(rounds.at[r], inc=1, device_id=device_id, device_id_type=MESH)

    def hear(r):
        pl.semaphore_wait(rounds.at[r], 6)

    spread_word(0)
    lax.fori_loop(0, 8, chunk, 0)
    hear(2)
    spread_word(3)
    stage2(kt_ref, ct, pos, cx)
    hear(3)
    spread_word(4)

    binning(pos, cx, away, 2 * (1 - core))
    swap = remote(away, came, core_sems.at[0], core_sems.at[1], sibling)
    swap.start()
    hear(4)
    spread_word(5)

    def plane_copy(d):
        px, py, pz, pc = plane_peer(d)
        return remote(plane_out.at[px * NY + py], plane_in.at[d], plane_send.at[d], plane_recv.at[d],
                      device(px, py, pz, pc))

    def merge(d, _):
        at = pl.ds(pl.multiple_of(d * 32, 32), 32)
        v = split_counts(keep[at, :] + came[at, :])
        keep[at, :] = v
        plane_out[d] = v.astype(bf16)
        return 0

    far_first = sorted(range(1, NX * NY), key=lambda d: -hops(d // NY, NX) - hops(d % NY, NY))
    for piece in range(2):
        half = 1 - x // 2 if piece == 0 else x // 2
        at = pl.multiple_of(256 * half, 256)
        binning(pos, cx, keep.at[pl.ds(at, 256)], 2 * core + half)
        if piece == 0:
            swap.wait()
        lax.fori_loop(8 * half, 8 * half + 8, merge, 0)
        for d in far_first:
            @pl.when(plane_peer(d)[0] // 2 == half)
            def _():
                plane_copy(d).start()

        if piece == 0:
            hear(5)
            spread_word(6)

    def take_plane(d, acc):
        plane_copy(d).wait()
        return acc + plane_in[d].astype(f32)

    mine = keep[pl.ds(pl.multiple_of((x * NY + y) * 32, 32), 32), :]
    total = lax.fori_loop(1, NX * NY, take_plane, mine)
    for i in range(NZ):
        line_out[i] = total[2 * i:2 * i + 2]

    def line_copy(d):
        px, py, pz, pc = line_peer(d)
        return remote(line_out.at[pz], line_in.at[d], line_send.at[d], line_recv.at[d], device(px, py, pz, pc))

    hear(6)
    for d in sorted(range(1, NZ), key=lambda d: -hops(d, NZ)):
        line_copy(d).start()

    def take_line(d, acc):
        line_copy(d).wait()
        return acc + line_in[d]

    finish(lax.fori_loop(1, NZ, take_line, line_out[z]), out_ref)

    @pl.when(core == 0)
    def _():
        def drain(g, _):
            down_copy(g).wait_send()
            side_copy(g).wait_send()
            return 0

        lax.fori_loop(0, 8, drain, 0)

    @pl.when(core == 1)
    def _():
        def drain(g, _):
            up_copy(g).wait_send()
            return 0

        lax.fori_loop(0, 8, drain, 0)

    def drain(s, _):
        forward(2 * s + core).wait_send()
        return 0

    lax.fori_loop(0, 4, drain, 0)


def run(*args):
    vm = pltpu.VMEM
    dma = pltpu.SemaphoreType.DMA
    i32 = jnp.int32
    return pl.pallas_call(
        kernel, out_shape=jax.ShapeDtypeStruct((4, TL), f32),
        in_specs=[pl.BlockSpec(memory_space=pltpu.VMEM)] * 5,
        out_specs=pl.BlockSpec(memory_space=pltpu.VMEM),
        scratch_shapes=[
            vm((8, 512, 128), f32), vm((16, 128), i32), vm((64, 128), f32), vm((128, 128), f32),
            vm((8, 256, 128), bf16), vm((32, 64, 128), f32), vm((8, 256, 128), bf16), vm((8, 256, 128), bf16),
            vm((2, 2, 256, 128), bf16), vm((2, 32, 1024, 128), bf16), vm((2, 32, 256, 128), bf16),
            vm((64, 128), i32), vm((64, 128), i32), vm((64, 128), i32), vm((64, 128), i32),
            vm((512, 256), f32), vm((512, 256), f32), vm((512, 256), f32),
            vm((16, 32, 256), bf16), vm((16, 32, 256), bf16), vm((16, 2, 256), f32), vm((16, 2, 256), f32),
            dma((2,)), dma((8,)), dma((8,)), dma((8,)), dma((8,)), dma((8,)),
            pltpu.SemaphoreType.REGULAR((NZ // 2 - 1,)),
            dma((2,)), dma((16,)), dma((16,)), dma((16,)), dma((16,)),
        ],
        compiler_params=pltpu.CompilerParams(
            vmem_limit_bytes=60 * 2**20, collective_id=0, has_side_effects=True),
    )(*args)


def shards(spectra, mid_bin, off_bin, owner_slot):
    return run(spectra, mid_bin, off_bin, owner_slot, lag_matrix())[:, :NL].T


def solution(mesh):
    in_specs = (
        P(("blk", "grp"), None, None),
        P(None, ("blk", "grp"), None),
        P(None, ("blk", "grp"), None),
        P(),
    )
    return jax.shard_map(shards, mesh=mesh, in_specs=in_specs, out_specs=P(None, ("blk", "grp")), check_vma=False)
```

```python
import jax
import jax.numpy as jnp
import numpy as np
from jax import lax
from jax.experimental import pallas as pl
from jax.experimental.pallas import tpu as pltpu
from jax.sharding import PartitionSpec as P

LAG = 50
NOFF = 16
F = 501
W = 4
FP = 512
TL = 128
NL = 2 * LAG + 1
bf16, f32 = jnp.bfloat16, jnp.float32


def lag_matrix():
    freq = np.arange(F, dtype=np.float32)
    lags = (np.arange(NL) - LAG).astype(np.float32)
    angle = (np.float32(2.0 * np.pi) * freq[:, None] * lags[None, :] / np.float32(2 * (F - 1))).astype(np.float32)
    w = np.where((freq == 0) | (freq == F - 1), 1.0, 2.0).astype(np.float32) / np.sqrt(np.float32(W * F))
    k = np.zeros((TL, 2 * FP), np.float32)
    k[:NL, :F] = (w[:, None] * np.cos(angle)).T
    k[:NL, FP:FP + F] = (-w[:, None] * np.sin(angle)).T
    return jnp.asarray(k, bf16)


def spread(x_ref, rows_ref):
    for i in range(64):
        x = x_ref[i].astype(f32)
        for t in range(8):
            n = min(128, 2 * F - 128 * t)
            rows_ref[t, pl.ds(8 * i, W), pl.ds(0, n)] = x[:, 128 * t:128 * t + n]


def parts(rows_ref, q):
    lane = lax.broadcasted_iota(jnp.int32, (64, 128), 1)
    cut = F - FP + 128
    gap = FP - F
    out = []
    for w in range(W):
        def tile(t):
            return rows_ref[t, pl.ds(w, 64, stride=8), :]

        re = tile(q)
        im = jnp.where(lane < gap, pltpu.roll(tile(q + 3), gap, 1), pltpu.roll(tile(q + 4), gap, 1))
        if q == 3:
            re, im = jnp.where(lane < cut, re, 0.0), jnp.where(lane < cut, im, 0.0)
        out += [re, im]
    return out


def prep_tile(rows_ref, bt_ref, ag_ref, q):
    lane = lax.broadcasted_iota(jnp.int32, (64, 128), 1)
    xs = parts(rows_ref, q)
    for k in range(8):
        x = xs[k]
        y = jnp.transpose(jnp.concatenate([x, pltpu.roll(x, 96, 1)], 0)).astype(bf16)
        bt_ref[2 * q, pl.ds(k * 32, 32), :] = y[0:32]
        bt_ref[2 * q + 1, pl.ds(k * 32, 32), :] = y[64:96]
    for s in range(4):
        for h in range(2):
            acc = None
            for m in range(4):
                shift = (32 * (m - s)) % 128
                v = xs[4 * h + m]
                v = pltpu.roll(v, shift, 1) if shift else v
                acc = v if acc is None else jnp.where(lane >= 32 * m, v, acc)
            ag_ref[(4 * q + s) * 2 + h] = acc


def weights(u_ref, v_ref, w_ref, gp, sign):
    lane = lax.broadcasted_iota(jnp.int32, (32, 128), 1)
    left = lane < 64
    sgn = jnp.where(left, 1.0, sign)
    for k in range(8):
        u = u_ref[gp, pl.ds(k * 32, 32), :].astype(f32)
        v = v_ref[gp, pl.ds(k * 32, 32), :].astype(f32)
        ur, vr = pltpu.roll(u, 64, 1), pltpu.roll(v, 64, 1)
        for n, val in ((0, jnp.where(left, u, vr)), (1, jnp.where(left, ur, v))):
            w_ref[n, 0, pl.ds(k * 32, 32), :] = val.astype(bf16)
            other = val * sgn if k % 2 == 0 else -(val * sgn)
            w_ref[n, 1, pl.ds((k ^ 1) * 32, 32), :] = other.astype(bf16)


def stage1(ag_ref, w_ref, ct_ref, gp):
    MI = 16
    row = lax.broadcasted_iota(jnp.int32, (32, 128), 0)
    lane = lax.broadcasted_iota(jnp.int32, (32, 128), 1)
    mask = jnp.where((lane & 31) == row, 1.0, 0.0).astype(bf16)

    def body(ib, _):
        for n in range(2):
            w = jnp.concatenate([w_ref[n, 0], w_ref[n, 1]], 1)
            for h in range(MH):
                parts = []
                for ii in range(MI):
                    halves = []
                    for q in range(2):
                        a = ag_ref[(2 * gp + n) * 2 + q, pl.ds((ib * MH + h) * MI + ii, 1), :]
                        a = jnp.broadcast_to(a, (16, 128)).astype(bf16)
                        halves.append(jnp.concatenate([a, a], 0) * mask)
                    parts.append(jnp.concatenate(halves, 1))
                e = jnp.concatenate(parts, 0)
                o = jnp.dot(e, w, preferred_element_type=f32).astype(bf16)
                r0 = pl.multiple_of((2 * gp + n) * 32, 32)
                for ii in range(MI):
                    p = ((ib * MH + h) * MI + ii) // 2
                    ct_ref[ii % 2, p, pl.ds(r0, 32), :] = o[ii * 32:ii * 32 + 32, 0:128]
                    ct_ref[ii % 2, p, pl.ds(r0 + FP, 32), :] = o[ii * 32:ii * 32 + 32, 128:256]
        return 0

    lax.fori_loop(0, 64 // (MI * MH), body, 0)


MH = 4


def stage2(kt_ref, ct_ref, pos_ref, cx_ref):
    sub = lax.broadcasted_iota(jnp.int32, (TL, 128), 0)
    count = (sub == NL) | (sub == NL + 1)

    def body(s, _):
        for u in range(8):
            ip = 8 * s + u
            w = jnp.concatenate([ct_ref[0, ip], ct_ref[1, ip]], 1)
            c = jnp.dot(kt_ref[...], w, preferred_element_type=f32)
            for h in range(2):
                row = pos_ref[pl.ds(2 * ip + h, 1), :]
                ch = jnp.where(count, 1.0, c[:, h * 128:h * 128 + 128]).astype(bf16)
                bit = (row & 1).astype(f32)
                bit = jnp.broadcast_to(bit, (TL, 128)).astype(bf16)
                hi = ch * bit
                cx_ref[h, ip, pl.ds(0, TL), :] = ch - hi
                cx_ref[h, ip, pl.ds(TL, TL), :] = hi
        return 0

    lax.fori_loop(0, 4, body, 0)


def lookup(slot_ref, tab_ref, bins_ref, pos_ref):
    for r in range(16):
        tab_ref[pl.ds(r, 1), :] = slot_ref[pl.ds(128 * r, 128)].reshape(1, 128)
    p = tab_ref[...]
    core, x, y = (p >> 4) & 1, (p >> 2) & 3, p >> 9
    z, k = (p >> 5) & 15, p & 3
    tab = core * 1024 + x * 256 + y * 64 + z * 4 + k
    tt = jnp.concatenate([(tab & 255).astype(f32), (tab >> 8).astype(f32)], 0).astype(bf16)
    sub = lax.broadcasted_iota(jnp.int32, (128, 256), 0)
    s16 = lax.broadcasted_iota(jnp.int32, (16, 256), 0)

    def body(s, _):
        for u in range(8):
            t = 16 * s + 2 * u
            b = jnp.concatenate([bins_ref[pl.ds(t, 1), :], bins_ref[pl.ds(t + 1, 1), :]], 1)
            oh = jnp.where(sub == (b & 127), 1.0, 0.0).astype(bf16)
            v = jnp.dot(tt, oh, preferred_element_type=f32)
            full = v[:16] + 256.0 * v[16:]
            p = jnp.sum(jnp.where(s16 == (b >> 7), full, 0.0), axis=0, keepdims=True).astype(jnp.int32)
            pos_ref[pl.ds(t, 1), :] = p[:, :128]
            pos_ref[pl.ds(t + 1, 1), :] = p[:, 128:]
        return 0

    lax.fori_loop(0, 4, body, 0)


def pair_bins(mid_ref, off_ref, upper, s0, s1, ubin, vbin):
    s0[...] = jnp.zeros_like(s0)
    s1[...] = jnp.zeros_like(s1)
    s0[:, pl.ds(0, 64)] = (mid_ref[0] * NOFF + off_ref[0]).astype(f32)
    s1[pl.ds(0, 64), pl.ds(0, 64)] = (mid_ref[1] * NOFF + off_ref[1]).astype(f32)
    near, far = s0[...], s1[...]
    ubin[...] = jnp.where(upper, far[0:64], near).astype(jnp.int32)
    vbin[...] = pltpu.roll(jnp.where(upper, near, jnp.transpose(far)[0:64]), 64, 1).astype(jnp.int32)


def binning(pos_ref, cx_ref, acc_ref, base):
    n = acc_ref.shape[0] // 256
    sub = lax.broadcasted_iota(jnp.int32, (256, 128), 0).astype(f32).astype(bf16)
    one, zero = jnp.ones((), bf16), jnp.zeros((), bf16)

    def body(s, _):
        lhs, rhs = [], []
        for u in range(KB):
            t = KB * s + u
            for q in range(2):
                a = pos_ref[pl.ds(2 * t + q, 1), :] >> 1
                lo, hi = a & 255, a >> 8
                col = []
                for h in range(n):
                    key = jnp.where(hi == base + h, lo, -1).astype(f32)
                    key = jnp.broadcast_to(key, (256, 128)).astype(bf16)
                    col.append(jnp.where(sub == key, one, zero))
                lhs.append(jnp.concatenate(col, 0))
                rhs.append(cx_ref[q, t])
        o = lax.dot_general(jnp.concatenate(lhs, 1), jnp.concatenate(rhs, 1), (((1,), (1,)), ((), ())), preferred_element_type=f32)
        acc_ref[...] = acc_ref[...] + o
        return 0

    acc_ref[...] = jnp.zeros_like(acc_ref)
    lax.fori_loop(0, 32 // KB, body, 0)


KB = 16


def finish(total, out_ref):
    for r in range(2):
        for h in range(2):
            out_ref[pl.ds(2 * r + h, 1), :] = total[r:r + 1, h * TL:h * TL + TL]
    t = out_ref[...]
    number = t[:, NL:NL + 1] + t[:, NL + 1:NL + 2]
    out_ref[...] = t / jnp.sqrt(jnp.maximum(number, 1.0))


NX, NY, NZ = 4, 4, 16
MESH = pl.DeviceIdType.MESH


def place():
    blk = lax.axis_index("blk")
    return lax.axis_index("grp"), blk // (2 * NZ), lax.rem(blk // 2, NZ), lax.rem(blk, 2)


def device(x, y, z, core):
    return {"blk": (y * NZ + z) * 2 + core, "grp": x}


def plane_peer(d):
    x, y, z, core = place()
    return lax.rem(x + d // NY, NX), lax.rem(y + lax.rem(d, NY), NY), z, core


def line_peer(d):
    x, y, z, core = place()
    return x, y, lax.rem(z + d, NZ), core


def chip_neighbour(by, core):
    n = lax.axis_size("blk")
    chip = lax.axis_index("blk") // 2
    return {"blk": lax.rem(chip + by + n // 2, n // 2) * 2 + core, "grp": lax.axis_index("grp")}


def torus_neighbours():
    x, y, z, core = place()
    for by in (1, -1):
        yield device(lax.rem(x + by + NX, NX), y, z, core)
        yield device(x, lax.rem(y + by + NY, NY), z, core)
        yield device(x, y, lax.rem(z + by + NZ, NZ), core)


def greet():
    barrier = pltpu.get_barrier_semaphore()
    x, y, z, core = place()
    near = [device(x, y, z, 1 - core)]
    near += [chip_neighbour(by, c) for by in (1, -1) for c in range(2)]
    near += list(torus_neighbours())
    for device_id in near:
        pl.semaphore_signal(barrier, inc=1, device_id=device_id, device_id_type=MESH)
    return len(near)


def split_counts(v):
    lane = lax.rem(lax.broadcasted_iota(jnp.int32, v.shape, len(v.shape) - 1), TL)
    high = jnp.floor(v * (1.0 / 128.0)) * 128.0
    return jnp.where(lane == NL, high, jnp.where(lane == NL + 1, v - high, v))


def remote(src, dst, send, recv, to):
    return pltpu.make_async_remote_copy(
        src_ref=src, dst_ref=dst, send_sem=send, recv_sem=recv, device_id=to, device_id_type=MESH)


def hops(d, size):
    return min(d, size - d)


def kernel(x_ref, mid_ref, off_ref, slot_ref, kt_ref, out_ref,
           rows, tab, s0, s1, bt, ag, ub, vb, w, ct, cx, ubin, vbin, vin, pos, away, came, keep,
           plane_out, plane_in, line_out, line_in,
           bin_sems, send1, send2, fwd_send, u_recv, v_recv,
           rounds, core_sems, plane_send, plane_recv, line_send, line_recv):
    near = greet()
    x, y, z, core = place()
    sibling = device(x, y, z, 1 - core)
    spread(x_ref, rows)
    prep_tile(rows, bt, ag, 0)
    pair_bins(mid_ref, off_ref, core == 1, s0, s1, ubin, vbin)
    pl.semaphore_wait(pltpu.get_barrier_semaphore(), near)

    def bin_copy():
        return remote(vbin, vin, bin_sems.at[0], bin_sems.at[1], chip_neighbour(-1, 0))

    def up_copy(g):
        return remote(bt.at[g], ub.at[g], send1.at[g], u_recv.at[g], chip_neighbour(1, lax.rem(g, 2)))

    def side_copy(g):
        return remote(bt.at[g], vb.at[g], send1.at[g], v_recv.at[g], sibling)

    def down_copy(g):
        return remote(bt.at[g], vb.at[g], send2.at[g], v_recv.at[g], chip_neighbour(-1, 0))

    def forward(g):
        return remote(ub.at[g], ub.at[g], fwd_send.at[g], u_recv.at[g], sibling)

    @pl.when(core == 0)
    def _():
        bin_copy().start()

    for q in range(4):
        if q > 0:
            prep_tile(rows, bt, ag, q)

        @pl.when(core == 0)
        def _():
            for g in (2 * q, 2 * q + 1):
                down_copy(g).start()
                side_copy(g).start()

        @pl.when(core == 1)
        def _():
            for g in (2 * q, 2 * q + 1):
                up_copy(g).start()

    @pl.when(core == 0)
    def _():
        bin_copy().wait()

    @pl.when(core == 1)
    def _():
        vin[...] = vbin[...]

    ubin[...] = ubin[...] + vin[...]
    lookup(slot_ref, tab, ubin, pos)
    sign = jnp.where(core == 0, -1.0, 1.0)

    def chunk(s, _):
        first = 2 * (s // 2) + core
        g = jnp.where(lax.rem(s, 2) == 0, first, 4 * (s // 2) + 1 - first)
        forward(g).wait_recv()

        @pl.when(lax.rem(s, 2) == 0)
        def _():
            forward(g).start()

        side_copy(g).wait_recv()
        weights(ub, vb, w, g, sign)
        stage1(ag, w, ct, g)

        @pl.when(lax.rem(s, 3) == 2)
        def _():
            hear(s // 3)
            spread_word(s // 3 + 1)

        return 0

    def spread_word(r):
        for device_id in torus_neighbours():
            pl.semaphore_signal(rounds.at[r], inc=1, device_id=device_id, device_id_type=MESH)

    def hear(r):
        pl.semaphore_wait(rounds.at[r], 6)

    spread_word(0)
    lax.fori_loop(0, 8, chunk, 0)
    hear(2)
    spread_word(3)
    stage2(kt_ref, ct, pos, cx)
    hear(3)
    spread_word(4)

    def half_of(piece):
        return lax.rem(1 - x // 2 + piece, 2)

    def swap(piece):
        at = pl.ds(pl.multiple_of(256 * half_of(piece), 256), 256)
        return remote(away.at[at], came.at[at], core_sems.at[piece], core_sems.at[2 + piece], sibling)

    def give(piece, _):
        half = half_of(piece)
        at = pl.multiple_of(256 * half, 256)
        binning(pos, cx, away.at[pl.ds(at, 256)], 2 * (1 - core) + half)
        swap(piece).start()
        return 0

    lax.fori_loop(0, 2, give, 0)
    hear(4)
    spread_word(5)

    def plane_copy(d):
        px, py, pz, pc = plane_peer(d)
        return remote(plane_out.at[px * NY + py], plane_in.at[d], plane_send.at[d], plane_recv.at[d],
                      device(px, py, pz, pc))

    def merge(d, _):
        at = pl.ds(pl.multiple_of(d * 32, 32), 32)
        v = split_counts(keep[at, :] + came[at, :])
        keep[at, :] = v
        plane_out[d] = v.astype(bf16)
        return 0

    far_first = sorted(range(1, NX * NY), key=lambda d: -hops(d // NY, NX) - hops(d % NY, NY))
    for piece in range(2):
        half = half_of(piece)
        at = pl.multiple_of(256 * half, 256)
        binning(pos, cx, keep.at[pl.ds(at, 256)], 2 * core + half)
        swap(piece).wait()
        lax.fori_loop(8 * half, 8 * half + 8, merge, 0)
        for d in far_first:
            @pl.when(plane_peer(d)[0] // 2 == half)
            def _():
                plane_copy(d).start()

        if piece == 0:
            hear(5)
            spread_word(6)

    def take_plane(d, acc):
        plane_copy(d).wait()
        return acc + plane_in[d].astype(f32)

    mine = keep[pl.ds(pl.multiple_of((x * NY + y) * 32, 32), 32), :]
    total = lax.fori_loop(1, NX * NY, take_plane, mine)
    for i in range(NZ):
        line_out[i] = total[2 * i:2 * i + 2]

    def line_copy(d):
        px, py, pz, pc = line_peer(d)
        return remote(line_out.at[pz], line_in.at[d], line_send.at[d], line_recv.at[d], device(px, py, pz, pc))

    hear(6)
    for d in sorted(range(1, NZ), key=lambda d: -hops(d, NZ)):
        line_copy(d).start()

    def take_line(d, acc):
        line_copy(d).wait()
        return acc + line_in[d]

    finish(lax.fori_loop(1, NZ, take_line, line_out[z]), out_ref)

    @pl.when(core == 0)
    def _():
        def drain(g, _):
            down_copy(g).wait_send()
            side_copy(g).wait_send()
            return 0

        lax.fori_loop(0, 8, drain, 0)

    @pl.when(core == 1)
    def _():
        def drain(g, _):
            up_copy(g).wait_send()
            return 0

        lax.fori_loop(0, 8, drain, 0)

    def drain(s, _):
        forward(2 * s + core).wait_send()
        return 0

    lax.fori_loop(0, 4, drain, 0)


def run(*args):
    vm = pltpu.VMEM
    dma = pltpu.SemaphoreType.DMA
    i32 = jnp.int32
    return pl.pallas_call(
        kernel, out_shape=jax.ShapeDtypeStruct((4, TL), f32),
        in_specs=[pl.BlockSpec(memory_space=pltpu.VMEM)] * 5,
        out_specs=pl.BlockSpec(memory_space=pltpu.VMEM),
        scratch_shapes=[
            vm((8, 512, 128), f32), vm((16, 128), i32), vm((64, 128), f32), vm((128, 128), f32),
            vm((8, 256, 128), bf16), vm((32, 64, 128), f32), vm((8, 256, 128), bf16), vm((8, 256, 128), bf16),
            vm((2, 2, 256, 128), bf16), vm((2, 32, 1024, 128), bf16), vm((2, 32, 256, 128), bf16),
            vm((64, 128), i32), vm((64, 128), i32), vm((64, 128), i32), vm((64, 128), i32),
            vm((512, 256), f32), vm((512, 256), f32), vm((512, 256), f32),
            vm((16, 32, 256), bf16), vm((16, 32, 256), bf16), vm((16, 2, 256), f32), vm((16, 2, 256), f32),
            dma((2,)), dma((8,)), dma((8,)), dma((8,)), dma((8,)), dma((8,)),
            pltpu.SemaphoreType.REGULAR((NZ // 2 - 1,)),
            dma((4,)), dma((16,)), dma((16,)), dma((16,)), dma((16,)),
        ],
        compiler_params=pltpu.CompilerParams(
            vmem_limit_bytes=60 * 2**20, collective_id=0, has_side_effects=True),
    )(*args)


def shards(spectra, mid_bin, off_bin, owner_slot):
    return run(spectra, mid_bin, off_bin, owner_slot, lag_matrix())[:, :NL].T


def solution(mesh):
    in_specs = (
        P(("blk", "grp"), None, None),
        P(None, ("blk", "grp"), None),
        P(None, ("blk", "grp"), None),
        P(),
    )
    return jax.shard_map(shards, mesh=mesh, in_specs=in_specs, out_specs=P(None, ("blk", "grp")), check_vma=False)
```
